32 devices in a mesh: lat: 4 (over z), lon: 8 (over y, x, core).
Axes of the slice: x: 2, y: 2, z: 4, core: 2. Of those that a mesh axis runs over, the one named last changes fastest.
Arguments:
- winds: bfloat16 [16, 32, 3, 40, 128], P('lat', 'lon'), may hold values from -6 to 6
- positions: float32 [4096, 3, 128], P(('lat', 'lon')), may hold values from 0 to 39, as said below
- velocity: float32 [4096, 3, 128], P(('lat', 'lon')), may hold values from -6 to 6
- increments: float32 [4096, 3, 128], P(('lat', 'lon')), may hold values from -6 to 6
- mass: float32 [4096, 8, 128], P(('lat', 'lon')), may hold values from 0.1 to 1
- requests: int32 [32, 32, 2], P(('lat', 'lon')), may hold values from 0 to 15
- block_slots: int32 [4096, 1], P(('lat', 'lon')), may hold values from 0 to 63; in each aligned block of 128 rows (0 to 127, 128 to 255, ...) at most 8 rows name the same one
- destinations: int32 [4096, 1], P(('lat', 'lon')), may hold values from 0 to 31; in each aligned block of 128 rows (0 to 127, 128 to 255, ...) at most 8 rows name the same one
- cell_keys: int32 [4096, 128], P(('lat', 'lon')), may hold values from 0 to 2047, as said below
Outputs:
- moved: float32 [4096, 3, 128], P(('lat', 'lon'))
- turbulence: float32 [4096, 3, 128], P(('lat', 'lon'))
- concentration: float32 [16, 32, 8, 40, 128], P('lat', 'lon')
The draws below stay inside these ranges and needn't reach their ends.
Inputs may be any that keep to these rules, and one draw needn't show every extreme that they name: `positions`: component 0 (cell row) lies in 0 to 7, component 1 (cell column) in 0 to 15, component 2 (level) in 0 to 39. requests[o, t, k] names a met block of tile t by its local number. `block_slots`: slot k stands for the (k % 2)-th request that the owner sends to tile k // 2; of the 128 blocks of one owner at most 8 have the same slot, and on some owners one slot gets exactly 8. `destinations`: of the 128 blocks of one owner at most 8 have the same destination; on some owners one destination gets exactly 8. `cell_keys`: a key is (local met block) * 128 + cell of the destination tile; all keys of one particle block lie in one met block.
All inputs are finite; a program needn't handle non-finite values.
Results may differ from the reference program's by a relative error of at most 0.0027.
Values may be sent and summed in bfloat16 or wider, within the bound.
A program may use at most 64 MiB of HBM per device.

```python
import math
import jax
import jax.numpy as jnp
import numpy as np
from jax import lax

BY = 8
BX = 16
MBC = 128
LEV = 40
S = 8
BLK = 128
MBR = 4
MBK = 4
MB = 16
Q = 2
PB = 128
CAP = 8
BLOCKS = 4096
N_LAT = 4
N_LON = 8
DEVICES = 32


def draw_positions(key, part):
    unit = jax.random.uniform(jax.random.fold_in(key, 11), (BLOCKS, 3, BLK), jnp.float32)
    upper = jnp.array([BY - 1, BX - 1, LEV - 1], jnp.float32)
    return unit * upper[None, :, None]


def draw_cell_keys(key, part):
    first, second = jax.random.split(jax.random.fold_in(key, 7))
    home = jax.random.randint(first, (BLOCKS, 1), 0, MBR * MBK)
    inside = jax.random.randint(second, (BLOCKS, BLK), 0, MBC)
    return (home * MBC + inside).astype(jnp.int32)


def plant(drawn, rng, least, largest):
    index_at = [jax.random.randint(jax.random.fold_in(rng, axis), (), 0, length) for axis, length in enumerate(drawn.shape)]
    longest = drawn.shape.index(max(drawn.shape))
    neighbour = index_at[:longest] + [(index_at[longest] + 1) % drawn.shape[longest]] + index_at[longest + 1:]
    return drawn.at[tuple(index_at)].set(least).at[tuple(neighbour)].set(largest)


def block_levels(rng, shape, pieces, low, top_value):
    def one(dim, parts):
        heights = jax.random.uniform(jax.random.fold_in(jax.random.fold_in(rng, 6), dim), (parts,), jnp.float32, low / len(pieces), top_value / len(pieces))
        return jnp.repeat(jnp.exp(heights), shape[dim] // parts).reshape((-1,) + (1,) * (len(shape) - dim - 1))

    gain = one(*pieces[0])
    for cut in pieces[1:]:
        gain = gain * one(*cut)
    return gain


def shared_out(own_key, own, number, rows, count, top, most, lean):
    order = jax.random.permutation(own_key, count)
    heavy_load, ordinary = load_shares(count, rows * top, most, lean, True), load_shares(count, rows * top, most, lean, False)
    places = jnp.arange(count)

    def named(lengths, rotation):
        used = int((lengths > 0).sum())
        fixed = max(1, used // 4)
        shifted = fixed + (places - fixed + rotation * (used - fixed)) % max(1, count - fixed)
        return jnp.zeros((count,), jnp.int32).at[order[jnp.where(places < fixed, places, shifted)]].set(jnp.asarray(lengths, jnp.int32))

    lengths = jnp.where(number % 4 == 0, named(heavy_load, number // 4), named(ordinary, number - number // 4 - 1))
    mixed = jax.random.permutation(jax.random.fold_in(own, 3), count)
    donor, sink = mixed[0:count // 2 * 2:2], mixed[1:count // 2 * 2:2]
    margin = jnp.minimum(lengths[donor] - 1, most - lengths[sink]) // 2
    margin = jnp.where((donor == order[0]) | (sink == order[0]) | (lengths[sink] == 0), 0, jnp.maximum(margin, 0))
    shifted = jax.random.randint(jax.random.fold_in(own, 4), (count // 2,), 0, 1 << 20) % (margin + 1)
    lengths = lengths.at[donor].add(-shifted).at[sink].add(shifted)
    items = jnp.searchsorted(jnp.cumsum(lengths), jnp.arange(rows * top), side="right").astype(jnp.int32)
    grid = items.reshape(top, rows).T
    grid = grid[jax.random.permutation(jax.random.fold_in(own, 1), rows)]
    rotation = jax.random.randint(jax.random.fold_in(own, 2), (rows, 1), 0, top)
    return jnp.take_along_axis(grid, (jnp.arange(top)[None, :] + rotation) % top, axis=1)


def load_shares(count, total, limit, skew, full):
    weights = [(1 << 20) // math.isqrt(grade ** skew) + 1 for grade in range(1, count + 1)]
    largest = limit if full else min(limit, max(-(-total // count), total * weights[0] // sum(weights)))
    least = 1 if total - largest >= count - 1 else 0
    counts, rest = [largest] + [least] * (count - 1), total - largest - least * (count - 1)
    while rest > 0:
        free = [i for i in range(1, count) if counts[i] < largest] or [i for i in range(1, count) if counts[i] < limit]
        whole, budget = sum([weights[i] for i in free]), rest
        for i in free:
            addition = min(limit - counts[i], max(1, budget * weights[i] // whole), rest)
            counts[i] = counts[i] + addition
            rest = rest - addition
    return np.array(counts)


def normal_values(stream_key, extent, deviation, limit, pieces=(), kind=jnp.bfloat16):
    gain = block_levels(stream_key, extent, pieces, -0.22, 0.18) if pieces else 1.0
    values = jax.random.normal(stream_key, extent, jnp.float32) * deviation * gain
    return jnp.minimum(jnp.maximum(values, -limit), limit).astype(kind)


def setup_inputs(seed: int = 0) -> dict:
    streams_of = jax.random.split(jax.random.key(seed), 10)
    winds = normal_values(streams_of[0], (MBR * N_LAT, MBK * N_LON, 3, LEV, MBC), 1.0, 6.0, ((0, 4), (1, 8)))
    positions = draw_positions(jax.random.fold_in(streams_of[9], 71), 0)
    velocity = normal_values(streams_of[2], (BLOCKS, 3, BLK), 1.0, 6.0, ((0, 32),), jnp.float32)
    increments = normal_values(streams_of[3], (BLOCKS, 3, BLK), 1.0, 6.0, ((0, 32),), jnp.float32)
    mass = jnp.clip(jnp.exp(math.log(1.0) - 2.3025851 * jax.random.uniform(streams_of[4], (BLOCKS, S, BLK), jnp.float32) ** block_levels(streams_of[4], (BLOCKS, S, BLK), ((0, 32),), -0.2, 0.2)), 0.1, 1.0)
    requests = plant(jax.random.randint(streams_of[5], (DEVICES, DEVICES, Q), 0, MB), jax.random.fold_in(streams_of[5], 1), 0, MB - 1).astype(jnp.int32)
    block_slots_keys = jax.random.split(jax.random.fold_in(streams_of[6], 1), BLOCKS // PB)
    block_slots_turns = jax.random.permutation(jax.random.fold_in(streams_of[6], 3), BLOCKS // PB)
    block_slots = jax.vmap(lambda own, number: shared_out(jax.random.fold_in(streams_of[6], 2), own, number, PB, DEVICES * Q, 1, CAP, 2))(block_slots_keys, block_slots_turns).reshape((BLOCKS, 1))
    destinations_keys = jax.random.split(jax.random.fold_in(streams_of[7], 1), BLOCKS // PB)
    destinations_turns = jax.random.permutation(jax.random.fold_in(streams_of[7], 3), BLOCKS // PB)
    destinations = jax.vmap(lambda own, number: shared_out(jax.random.fold_in(streams_of[7], 2), own, number, PB, DEVICES, 1, CAP, 2))(destinations_keys, destinations_turns).reshape((BLOCKS, 1))
    cell_keys = draw_cell_keys(jax.random.fold_in(streams_of[9], 71), 0)
    return dict(winds=winds, positions=positions, velocity=velocity, increments=increments, mass=mass, requests=requests, block_slots=block_slots, destinations=destinations, cell_keys=cell_keys)


DECAY = 0.8
KICK = 0.6
STEP = 0.5


def corner(coord, top):
    base = jnp.clip(jnp.floor(coord), 0, top - 1).astype(jnp.int32)
    frac = coord - base.astype(coord.dtype)
    return base, frac


def reference(winds, positions, velocity, increments, mass, requests, block_slots, destinations, cell_keys):
    devices = N_LAT * N_LON
    block_cols = MBK * N_LON
    table = winds.reshape(-1)
    conc = jnp.zeros((MBR * N_LAT * block_cols * S * LEV * MBC,), jnp.float32)
    upper = jnp.array([BY - 1, BX - 1, LEV - 1], jnp.float32)

    def owner_step(total, items):
        pos, vel, noise, share, asked, slots, target, keys = items
        source = slots // Q
        local = asked[source, slots % Q]
        grow = (source // N_LON) * MBR + local // MBK
        gcol = (source % N_LON) * MBK + local % MBK
        blockid = (grow * block_cols + gcol)[:, None]
        row0, fy = corner(pos[:, 0], BY - 1)
        col0, fx = corner(pos[:, 1], BX - 1)
        lev0, fz = corner(pos[:, 2], LEV - 1)
        wz0 = (1.0 - fz).astype(jnp.bfloat16).astype(jnp.float32)
        wz1 = fz.astype(jnp.bfloat16).astype(jnp.float32)
        winds_at = []
        for comp in range(3):
            acc = jnp.zeros(fy.shape, jnp.float32)
            for di in range(2):
                hy = (1.0 - fy) if di == 0 else fy
                for dj in range(2):
                    hx = (1.0 - fx) if dj == 0 else fx
                    cell = (row0 + di) * BX + col0 + dj
                    base = (blockid * 3 + comp) * LEV
                    low = table[(base + lev0) * MBC + cell].astype(jnp.float32)
                    high = table[(base + lev0 + 1) * MBC + cell].astype(jnp.float32)
                    acc = acc + (hy * hx) * (wz0 * low + wz1 * high)
            winds_at.append(acc)
        wind = jnp.stack(winds_at, axis=1)
        new_vel = DECAY * vel + KICK * noise
        new_pos = jnp.clip(pos + STEP * (wind + new_vel), 0.0, upper[None, :, None])
        lz, tz = corner(new_pos[:, 2], LEV - 1)
        dest = target[:, 0][:, None]
        home = keys // MBC
        cell = keys % MBC
        grow = (dest // N_LON) * MBR + home // MBK
        gcol = (dest % N_LON) * MBK + home % MBK
        base = (grow * block_cols + gcol) * S
        indices = []
        values = []
        for s in range(S):
            for dl in range(2):
                weight = (1.0 - tz) if dl == 0 else tz
                indices.append(((base + s) * LEV + lz + dl) * MBC + cell)
                values.append((share[:, s] * weight).astype(jnp.bfloat16).astype(jnp.float32))
        total = total.at[jnp.stack(indices).reshape(-1)].add(jnp.stack(values).reshape(-1))
        return total, (new_pos, new_vel)

    items = (positions.reshape(devices, PB, 3, BLK), velocity.reshape(devices, PB, 3, BLK),
             increments.reshape(devices, PB, 3, BLK), mass.reshape(devices, PB, S, BLK),
             requests, block_slots.reshape(devices, PB), destinations.reshape(devices, PB, 1),
             cell_keys.reshape(devices, PB, BLK))
    conc, (new_pos, new_vel) = lax.scan(owner_step, conc, items)
    moved = new_pos.reshape(BLOCKS, 3, BLK)
    turbulence = new_vel.reshape(BLOCKS, 3, BLK)
    concentration = conc.reshape(MBR * N_LAT, block_cols, S, LEV, MBC)
    return moved, turbulence, concentration
```

```python
import functools

import jax
import jax.numpy as jnp
from jax import lax
from jax.experimental import pallas as pl
from jax.experimental.pallas import tpu as pltpu
from jax.sharding import PartitionSpec as P

BY = 8
BX = 16
MBC = 128
LEV = 40
S = 8
BLK = 128
MBR = 4
MBK = 4
Q = 2
MB = MBR * MBK

DECAY = 0.8
KICK = 0.6
STEP = 0.5

FULL = 65535.0
GUST = 6.1
VMEM = pl.BlockSpec(memory_space=pltpu.VMEM)
SMEM = pl.BlockSpec(memory_space=pltpu.SMEM)


def up8(rows):
    return -(-rows // 8) * 8


def hat(offset):
    return jnp.maximum(0.0, 1.0 - jnp.abs(offset))


def low(word):
    return (word & 0xFFFF).astype(jnp.float32)


def high(word):
    return lax.shift_right_logical(word, 16).astype(jnp.float32)


def code(value, scale):
    return (value * scale + 0.5).astype(jnp.int32)


def span(count, unroll, step):
    def group(i, carry):
        for j in range(unroll):
            step(i * unroll + j)
        return carry

    lax.fori_loop(0, count // unroll, group, 0)


def pack_kernel(
    dims, slots, targets, requests, positions, mass, keys,
    spot_msg, mass_msg, spot_place, mass_place, spot_count, mass_count,
):
    n, blocks, room, spot_rows, mass_rows = dims
    entries = Q * room
    spot_head = entries + entries // 2
    mass_head = 4 * room + room // 2
    lanes = lax.broadcasted_iota(jnp.int32, (1, BLK), 1)
    spot_msg[...] = jnp.zeros_like(spot_msg)
    mass_msg[...] = jnp.zeros_like(mass_msg)

    def clear(t, carry):
        spot_count[t] = 0
        mass_count[t] = 0
        return carry

    lax.fori_loop(0, n, clear, 0)
    rows3 = lax.broadcasted_iota(jnp.int32, (3, BLK), 0)
    scale = jnp.where(
        rows3 == 0, FULL / (BY - 1), jnp.where(rows3 == 1, FULL / (BX - 1), FULL / (LEV - 1))
    )

    def one(b):
        slot = slots[b]
        t = slot // Q
        met = requests[slot]
        r = spot_count[t]
        spot_count[t] = r + 1
        spot_place[b] = t * entries + r
        codes = code(positions[b], scale)
        base = t * spot_rows
        spot_msg[pl.ds(base + r, 1), :] = codes[0:1] | (codes[1:2] << 16)
        z_row = pl.ds(base + entries + r // 2, 1)
        spot_msg[z_row, :] = spot_msg[z_row, :] | (codes[2:3] << (16 * (r & 1)))
        h_row = pl.ds(base + spot_head, 1)
        spot_msg[h_row, :] = jnp.where(
            lanes == r, met, jnp.where(lanes == entries, r + 1, spot_msg[h_row, :])
        )
        d = targets[b]
        q = mass_count[d]
        mass_count[d] = q + 1
        mass_place[b] = d * room + q
        shares = code(mass[b], FULL)
        words = shares[0:4] | (shares[4:8] << 16)
        base = d * mass_rows
        for j in range(4):
            mass_msg[pl.ds(base + 4 * q + j, 1), :] = words[j : j + 1]
        key = keys[pl.ds(b, 1), :]
        k_row = pl.ds(base + 4 * room + q // 2, 1)
        mass_msg[k_row, :] = mass_msg[k_row, :] | (key << (16 * (q & 1)))
        h_row = pl.ds(base + mass_head, 1)
        home = jnp.broadcast_to(key[:, 0:1], (1, BLK)) // MBC
        mass_msg[h_row, :] = jnp.where(
            lanes == q, home, jnp.where(lanes == room, q + 1, mass_msg[h_row, :])
        )

    span(blocks, 4, one)


def list_pairs(n, lane, head, todo, group):
    def source(o, at):
        pairs = (head[o, lane] + 1) // 2

        def put(k, at):
            todo[at] = o * 256 + k
            return at + 1

        return lax.fori_loop(0, pairs, put, at)

    return lax.fori_loop(0, n, source, 0)


def wind_kernel(dims, head, spots, tiles, back, todo):
    n, room, spot_rows, back_rows = dims
    entries = Q * room
    total = list_pairs(n, entries, head, todo, 2)
    levels = lax.broadcasted_iota(jnp.int32, (LEV, BLK), 0).astype(jnp.float32)
    cols = lax.broadcasted_iota(jnp.int32, (BX, BLK), 0).astype(jnp.float32)

    def sample(o, r, z):
        word = spots[pl.ds(o * spot_rows + r, 1), :]
        y = low(word) * ((BY - 1) / FULL)
        x = high(word) * ((BX - 1) / FULL)
        hx = hat(x - cols)
        flat = jnp.concatenate([hat(y - float(i)) * hx for i in range(BY)], axis=0)
        flat_hi = flat.astype(jnp.bfloat16)
        flat_lo = (flat - flat_hi.astype(jnp.float32)).astype(jnp.bfloat16)
        block = tiles[head[o, r]]
        seen = jnp.dot(block, flat_hi, preferred_element_type=jnp.float32) + jnp.dot(
            block, flat_lo, preferred_element_type=jnp.float32
        )
        wz = hat(z - levels).astype(jnp.bfloat16).astype(jnp.float32)
        codes = []
        for c in range(3):
            wind = jnp.sum(seen[c * LEV : (c + 1) * LEV] * wz, axis=0, keepdims=True)
            codes.append(code(wind + GUST, FULL / (2 * GUST)))
        back[pl.ds(o * back_rows + r, 1), :] = codes[0] | (codes[1] << 16)
        return codes[2]

    def pair(i):
        item = todo[i]
        o = item // 256
        k = item % 256
        word = spots[pl.ds(o * spot_rows + entries + k, 1), :]
        first = sample(o, 2 * k, low(word) * ((LEV - 1) / FULL))
        second = sample(o, 2 * k + 1, high(word) * ((LEV - 1) / FULL))
        back[pl.ds(o * back_rows + entries + k, 1), :] = first | (second << 16)

    lax.fori_loop(0, total, lambda i, c: (pair(i), c)[1], 0)


def move_kernel(
    dims, spot_place, mass_place, back, positions, velocity, increments,
    moved, turbulence, z_msg,
):
    n, blocks, room, back_rows, z_rows = dims
    entries = Q * room
    z_msg[...] = jnp.zeros_like(z_msg)
    rows3 = lax.broadcasted_iota(jnp.int32, (3, BLK), 0)
    upper = jnp.where(rows3 == 0, BY - 1.0, jnp.where(rows3 == 1, BX - 1.0, LEV - 1.0))

    def one(b):
        place = spot_place[b]
        t = place // entries
        r = place % entries
        word = back[pl.ds(t * back_rows + r, 1), :]
        word_z = back[pl.ds(t * back_rows + entries + r // 2, 1), :]
        up = lax.shift_right_logical(word_z, jnp.full_like(word_z, 16 * (r & 1)))
        wind = jnp.where(rows3 == 0, low(word), jnp.where(rows3 == 1, high(word), low(up)))
        wind = wind * (2 * GUST / FULL) - GUST
        drift = DECAY * velocity[b] + KICK * increments[b]
        turbulence[b] = drift
        new = jnp.clip(positions[b] + STEP * (wind + drift), 0.0, upper)
        moved[b] = new
        spot = mass_place[b]
        z_msg[pl.ds((spot // room) * z_rows + spot % room, 1), :] = new[2:3]

    span(blocks, 4, one)


def deposit_kernel(dims, head, shares, heights, out, todo):
    n, room, mass_rows, z_rows = dims
    out[...] = jnp.zeros_like(out)
    total = list_pairs(n, room, head, todo, 2)
    levels = lax.broadcasted_iota(jnp.int32, (LEV, BLK), 0).astype(jnp.float32)
    cells = lax.broadcasted_iota(jnp.int32, (MBC, BLK), 0)

    def add(o, q, key):
        inside = key % MBC
        vert = hat(heights[pl.ds(o * z_rows + q, 1), :] - levels)
        lows, highs = [], []
        for j in range(4):
            word = shares[pl.ds(o * mass_rows + 4 * q + j, 1), :]
            lows.append((low(word) * (1 / FULL)) * vert)
            highs.append((high(word) * (1 / FULL)) * vert)
        weights = jnp.concatenate(lows + highs, axis=0).astype(jnp.bfloat16)
        picks = jnp.where(inside == cells, 1.0, 0.0).astype(jnp.bfloat16)
        part = lax.dot_general(
            weights, picks, (((1,), (1,)), ((), ())), preferred_element_type=jnp.float32
        )
        home = head[o, q]
        out[home] += part

    def pair(i):
        item = todo[i]
        o = item // 256
        k = item % 256
        word = shares[pl.ds(o * mass_rows + 4 * room + k, 1), :]
        add(o, 2 * k, word & 0xFFFF)
        add(o, 2 * k + 1, lax.shift_right_logical(word, 16))

    lax.fori_loop(0, total, lambda i, c: (pair(i), c)[1], 0)


def swap(msg, n):
    shape = msg.shape
    msg = msg.reshape(n, -1, BLK)
    msg = lax.all_to_all(msg, ("lat", "lon"), split_axis=0, concat_axis=0, tiled=True)
    return msg.reshape(shape)


def body(
    winds, positions, velocity, increments, mass, requests, block_slots, destinations, cell_keys
):
    n = lax.axis_size("lat") * lax.axis_size("lon")
    blocks = positions.shape[0]
    room = 2 * blocks // n
    entries = Q * room
    spot_head = entries + entries // 2
    mass_head = 4 * room + room // 2
    spot_rows = up8(spot_head + 1)
    back_rows = up8(spot_head)
    mass_rows = up8(mass_head + 1)
    z_rows = up8(room)
    i32 = jnp.int32
    f32 = jnp.float32

    spot_msg, mass_msg, spot_place, mass_place = pl.pallas_call(
        functools.partial(pack_kernel, (n, blocks, room, spot_rows, mass_rows)),
        out_shape=(
            jax.ShapeDtypeStruct((n * spot_rows, BLK), i32),
            jax.ShapeDtypeStruct((n * mass_rows, BLK), i32),
            jax.ShapeDtypeStruct((blocks,), i32),
            jax.ShapeDtypeStruct((blocks,), i32),
        ),
        in_specs=[SMEM, SMEM, SMEM, VMEM, VMEM, VMEM],
        out_specs=(VMEM, VMEM, SMEM, SMEM),
        scratch_shapes=[pltpu.SMEM((n,), i32), pltpu.SMEM((n,), i32)],
        name="pack",
    )(
        block_slots.reshape(-1), destinations.reshape(-1), requests.reshape(-1),
        positions, mass, cell_keys,
    )
    spots = swap(spot_msg, n)
    shares = swap(mass_msg, n)
    spot_list = spots.reshape(n, spot_rows, BLK)[:, spot_head, :]
    back = pl.pallas_call(
        functools.partial(wind_kernel, (n, room, spot_rows, back_rows)),
        out_shape=jax.ShapeDtypeStruct((n * back_rows, BLK), i32),
        in_specs=[SMEM, VMEM, VMEM],
        out_specs=VMEM,
        scratch_shapes=[pltpu.SMEM((n * (entries // 2),), i32)],
        name="wind",
    )(spot_list, spots, winds.reshape(MB, 3 * LEV, MBC))
    back = swap(back, n)
    moved, turbulence, z_msg = pl.pallas_call(
        functools.partial(move_kernel, (n, blocks, room, back_rows, z_rows)),
        out_shape=(
            jax.ShapeDtypeStruct(positions.shape, f32),
            jax.ShapeDtypeStruct(positions.shape, f32),
            jax.ShapeDtypeStruct((n * z_rows, BLK), f32),
        ),
        in_specs=[SMEM, SMEM, VMEM, VMEM, VMEM, VMEM],
        out_specs=(VMEM, VMEM, VMEM),
        name="move",
    )(spot_place, mass_place, back, positions, velocity, increments)
    heights = swap(z_msg, n)
    mass_list = shares.reshape(n, mass_rows, BLK)[:, mass_head, :]
    total = pl.pallas_call(
        functools.partial(deposit_kernel, (n, room, mass_rows, z_rows)),
        out_shape=jax.ShapeDtypeStruct((MB, S * LEV, MBC), f32),
        in_specs=[SMEM, VMEM, VMEM],
        out_specs=VMEM,
        scratch_shapes=[pltpu.SMEM((n * max(1, room // 2),), i32)],
        name="deposit",
    )(mass_list, shares, heights)
    concentration = total.reshape(MBR, MBK, S, LEV, MBC)
    return (moved, turbulence, concentration)


def solution(mesh):
    rows = ("lat", "lon")
    in_specs = (
        P("lat", "lon", None, None, None),
        P(rows, None, None),
        P(rows, None, None),
        P(rows, None, None),
        P(rows, None, None),
        P(rows, None, None),
        P(rows, None),
        P(rows, None),
        P(rows, None),
    )
    out_specs = (
        P(rows, None, None),
        P(rows, None, None),
        P("lat", "lon", None, None, None),
    )
    return jax.shard_map(body, mesh=mesh, in_specs=in_specs, out_specs=out_specs, check_vma=False)
```

```python
import functools

import jax
import jax.numpy as jnp
from jax import lax
from jax.experimental import pallas as pl
from jax.experimental.pallas import tpu as pltpu
from jax.sharding import PartitionSpec as P

BY = 8
BX = 16
MBC = 128
LEV = 40
S = 8
BLK = 128
MBR = 4
MBK = 4
Q = 2
MB = MBR * MBK

DECAY = 0.8
KICK = 0.6
STEP = 0.5

FULL = 65535.0
GUST = 6.1
GROUP = 4
VMEM = pl.BlockSpec(memory_space=pltpu.VMEM)
SMEM = pl.BlockSpec(memory_space=pltpu.SMEM)


def up8(rows):
    return -(-rows // 8) * 8


def hat(offset):
    return jnp.maximum(0.0, 1.0 - jnp.abs(offset))


def low(word):
    return (word & 0xFFFF).astype(jnp.float32)


def high(word):
    return lax.shift_right_logical(word, 16).astype(jnp.float32)


def code(value, scale):
    return (value * scale + 0.5).astype(jnp.int32)


def span(count, unroll, step):
    def group(i, carry):
        for j in range(unroll):
            step(i * unroll + j)
        return carry

    lax.fori_loop(0, count // unroll, group, 0)


def pack_kernel(
    dims, slots, targets, requests, positions, mass, keys,
    spot_msg, mass_msg, spot_place, mass_place, spot_count, mass_count, yx, zs,
):
    n, blocks, room, spot_rows, mass_rows = dims
    entries = Q * room
    spot_head = entries + entries // 2
    mass_head = 4 * room + room // 2
    lanes = lax.broadcasted_iota(jnp.int32, (1, BLK), 1)
    spot_msg[...] = jnp.zeros_like(spot_msg)
    mass_msg[...] = jnp.zeros_like(mass_msg)
    yx[...] = code(positions[0], FULL / (BY - 1)) | (code(positions[1], FULL / (BX - 1)) << 16)
    zs[...] = code(positions[2], FULL / (LEV - 1))

    def clear(t, carry):
        spot_count[t] = 0
        mass_count[t] = 0
        return carry

    lax.fori_loop(0, n, clear, 0)

    def one(b):
        slot = slots[b]
        t = slot // Q
        met = requests[slot % Q, t]
        r = spot_count[t]
        spot_count[t] = r + 1
        spot_place[b] = t * entries + r
        base = t * spot_rows
        spot_msg[pl.ds(base + r, 1), :] = yx[pl.ds(b, 1), :]
        z_row = pl.ds(base + entries + r // 2, 1)
        spot_msg[z_row, :] = spot_msg[z_row, :] | (zs[pl.ds(b, 1), :] << (16 * (r & 1)))
        h_row = pl.ds(base + spot_head, 1)
        spot_msg[h_row, :] = jnp.where(
            lanes == r, met, jnp.where(lanes == entries, r + 1, spot_msg[h_row, :])
        )
        d = targets[b]
        q = mass_count[d]
        mass_count[d] = q + 1
        mass_place[b] = d * room + q
        shares = code(mass[b], FULL)
        words = shares[0:4] | (shares[4:8] << 16)
        base = d * mass_rows
        for j in range(4):
            mass_msg[pl.ds(base + 4 * q + j, 1), :] = words[j : j + 1]
        key = keys[pl.ds(b, 1), :]
        k_row = pl.ds(base + 4 * room + q // 2, 1)
        mass_msg[k_row, :] = mass_msg[k_row, :] | (key << (16 * (q & 1)))
        h_row = pl.ds(base + mass_head, 1)
        home = jnp.broadcast_to(key[:, 0:1], (1, BLK)) // MBC
        mass_msg[h_row, :] = jnp.where(
            lanes == q, home, jnp.where(lanes == room, q + 1, mass_msg[h_row, :])
        )

    span(blocks, 4, one)


def list_pairs(n, lane, head, todo, group):
    def source(o, at):
        pairs = (head[o, lane] + 1) // 2

        def put(k, at):
            todo[at] = o * 256 + k
            return at + 1

        return lax.fori_loop(0, pairs, put, at)

    total = lax.fori_loop(0, n, source, 0)
    for j in range(group - 1):
        todo[total + j] = 0
    return total


def wind_kernel(dims, head, spots, tiles, back, todo):
    n, room, spot_rows, back_rows = dims
    entries = Q * room
    total = list_pairs(n, entries, head, todo, GROUP)
    levels = lax.broadcasted_iota(jnp.int32, (LEV, BLK), 0).astype(jnp.float32)
    cols = lax.broadcasted_iota(jnp.int32, (BX, BLK), 0).astype(jnp.float32)

    def sample(o, r, z):
        word = spots[pl.ds(o * spot_rows + r, 1), :]
        y = low(word) * ((BY - 1) / FULL)
        x = high(word) * ((BX - 1) / FULL)
        hx = hat(x - cols)
        flat = jnp.concatenate([hat(y - float(i)) * hx for i in range(BY)], axis=0)
        flat_hi = flat.astype(jnp.bfloat16)
        flat_lo = (flat - flat_hi.astype(jnp.float32)).astype(jnp.bfloat16)
        block = tiles[head[o, r]]
        seen = jnp.dot(
            jnp.concatenate([block, block], axis=1),
            jnp.concatenate([flat_hi, flat_lo], axis=0),
            preferred_element_type=jnp.float32,
        )
        wz = hat(z - levels).astype(jnp.bfloat16).astype(jnp.float32)
        codes = []
        for c in range(3):
            wind = jnp.sum(seen[c * LEV : (c + 1) * LEV] * wz, axis=0, keepdims=True)
            codes.append(code(wind + GUST, FULL / (2 * GUST)))
        return codes[0] | (codes[1] << 16), codes[2]

    def several(i, carry):
        results = []
        for j in range(GROUP):
            item = todo[i * GROUP + j]
            o = item // 256
            k = item % 256
            word = spots[pl.ds(o * spot_rows + entries + k, 1), :]
            first, first_up = sample(o, 2 * k, low(word) * ((LEV - 1) / FULL))
            second, second_up = sample(o, 2 * k + 1, high(word) * ((LEV - 1) / FULL))
            results.append((o * back_rows, k, first, second, first_up | (second_up << 16)))
        for base, k, first, second, up in results:
            back[pl.ds(base + 2 * k, 1), :] = first
            back[pl.ds(base + 2 * k + 1, 1), :] = second
            back[pl.ds(base + entries + k, 1), :] = up
        return carry

    lax.fori_loop(0, (total + GROUP - 1) // GROUP, several, 0)


def move_kernel(
    dims, spot_place, mass_place, back, positions, velocity, increments,
    moved, turbulence, z_msg, yx, zs,
):
    n, blocks, room, back_rows, z_rows = dims
    entries = Q * room
    z_msg[...] = jnp.zeros_like(z_msg)

    def fetch(b):
        place = spot_place[b]
        t = place // entries
        r = place % entries
        yx[pl.ds(b, 1), :] = back[pl.ds(t * back_rows + r, 1), :]
        word = back[pl.ds(t * back_rows + entries + r // 2, 1), :]
        zs[pl.ds(b, 1), :] = lax.shift_right_logical(word, jnp.full_like(word, 16 * (r & 1)))

    span(blocks, 8, fetch)
    winds = (low(yx[...]), high(yx[...]), low(zs[...]))
    for c, top in enumerate((BY - 1.0, BX - 1.0, LEV - 1.0)):
        wind = winds[c] * (2 * GUST / FULL) - GUST
        drift = DECAY * velocity[c] + KICK * increments[c]
        turbulence[c] = drift
        moved[c] = jnp.clip(positions[c] + STEP * (wind + drift), 0.0, top)

    def post(b):
        spot = mass_place[b]
        z_msg[pl.ds((spot // room) * z_rows + spot % room, 1), :] = moved[2, pl.ds(b, 1), :]

    span(blocks, 8, post)


def exchange_kernel(n, n_lon, rows, src, dst, send, recv, local):
    me = lax.axis_index("lat") * n_lon + lax.axis_index("lon")
    barrier = pltpu.get_barrier_semaphore()

    def place(k):
        peer = lax.rem(me + k, n)
        return peer, (peer // n_lon, lax.rem(peer, n_lon))

    def greet(k, carry):
        pl.semaphore_signal(
            barrier, inc=1, device_id=place(k)[1], device_id_type=pl.DeviceIdType.MESH
        )
        return carry

    def copy(k):
        peer, where = place(k)
        return pltpu.make_async_remote_copy(
            src_ref=src.at[peer, pl.ds(0, rows)],
            dst_ref=dst.at[me, pl.ds(0, rows)],
            send_sem=send.at[k],
            recv_sem=recv.at[k],
            device_id=where,
            device_id_type=pl.DeviceIdType.MESH,
        )

    def begin(k, carry):
        copy(k).start()
        return carry

    def finish(k, carry):
        source = lax.rem(me - k + n, n)
        peer, where = place(k)
        copy(k).wait_send()
        pltpu.make_async_remote_copy(
            src_ref=src.at[peer, pl.ds(0, rows)],
            dst_ref=dst.at[source, pl.ds(0, rows)],
            send_sem=send.at[k],
            recv_sem=recv.at[k],
            device_id=where,
            device_id_type=pl.DeviceIdType.MESH,
        ).wait_recv()
        return carry

    own = pltpu.make_async_copy(src.at[me], dst.at[me], local)
    own.start()
    lax.fori_loop(1, n, greet, 0)
    pl.semaphore_wait(barrier, n - 1)
    lax.fori_loop(1, n, begin, 0)
    lax.fori_loop(1, n, finish, 0)
    own.wait()


def exchange(msg, rows, number):
    n_lon = lax.axis_size("lon")
    n = lax.axis_size("lat") * n_lon
    shape = msg.shape
    msg = msg.reshape(n, -1, BLK)
    return pl.pallas_call(
        functools.partial(exchange_kernel, n, n_lon, rows),
        out_shape=jax.ShapeDtypeStruct(msg.shape, msg.dtype),
        in_specs=[VMEM],
        out_specs=VMEM,
        scratch_shapes=[
            pltpu.SemaphoreType.DMA((n,)),
            pltpu.SemaphoreType.DMA((n,)),
            pltpu.SemaphoreType.DMA,
        ],
        compiler_params=pltpu.CompilerParams(collective_id=number, has_side_effects=True),
        name="exchange" + str(number),
    )(msg).reshape(shape)


def deposit_kernel(dims, head, shares, heights, out, todo):
    n, room, mass_rows, z_rows = dims
    out[...] = jnp.zeros_like(out)
    total = list_pairs(n, room, head, todo, 1)
    levels = lax.broadcasted_iota(jnp.int32, (LEV, BLK), 0).astype(jnp.float32)
    cells = lax.broadcasted_iota(jnp.int32, (MBC, BLK), 0)

    def add(o, q, key):
        inside = key % MBC
        vert = hat(heights[pl.ds(o * z_rows + q, 1), :] - levels)
        lows, highs = [], []
        for j in range(4):
            word = shares[pl.ds(o * mass_rows + 4 * q + j, 1), :]
            lows.append((low(word) * (1 / FULL)) * vert)
            highs.append((high(word) * (1 / FULL)) * vert)
        weights = jnp.concatenate(lows + highs, axis=0).astype(jnp.bfloat16)
        picks = jnp.where(inside == cells, 1.0, 0.0).astype(jnp.bfloat16)
        part = lax.dot_general(
            weights, picks, (((1,), (1,)), ((), ())), preferred_element_type=jnp.float32
        )
        home = head[o, q]
        out[home] += part

    def pair(i):
        item = todo[i]
        o = item // 256
        k = item % 256
        word = shares[pl.ds(o * mass_rows + 4 * room + k, 1), :]
        add(o, 2 * k, word & 0xFFFF)
        add(o, 2 * k + 1, lax.shift_right_logical(word, 16))

    lax.fori_loop(0, total, lambda i, c: (pair(i), c)[1], 0)


def swap(msg, n):
    shape = msg.shape
    msg = msg.reshape(n, -1, BLK)
    msg = lax.all_to_all(msg, ("lat", "lon"), split_axis=0, concat_axis=0, tiled=True)
    return msg.reshape(shape)


def body(
    winds, positions, velocity, increments, mass, requests, block_slots, destinations, cell_keys
):
    n = lax.axis_size("lat") * lax.axis_size("lon")
    blocks = positions.shape[0]
    room = 2 * blocks // n
    entries = Q * room
    spot_head = entries + entries // 2
    mass_head = 4 * room + room // 2
    spot_rows = up8(spot_head + 1)
    back_rows = up8(spot_head)
    mass_rows = up8(mass_head + 1)
    z_rows = up8(room)
    i32 = jnp.int32
    f32 = jnp.float32

    positions, velocity, increments = (
        each.transpose(1, 0, 2) for each in (positions, velocity, increments)
    )
    spot_msg, mass_msg, spot_place, mass_place = pl.pallas_call(
        functools.partial(pack_kernel, (n, blocks, room, spot_rows, mass_rows)),
        out_shape=(
            jax.ShapeDtypeStruct((n * spot_rows, BLK), i32),
            jax.ShapeDtypeStruct((n * mass_rows, BLK), i32),
            jax.ShapeDtypeStruct((blocks,), i32),
            jax.ShapeDtypeStruct((blocks,), i32),
        ),
        in_specs=[SMEM, SMEM, SMEM, VMEM, VMEM, VMEM],
        out_specs=(VMEM, VMEM, SMEM, SMEM),
        scratch_shapes=[
            pltpu.SMEM((n,), i32),
            pltpu.SMEM((n,), i32),
            pltpu.VMEM((blocks, BLK), i32),
            pltpu.VMEM((blocks, BLK), i32),
        ],
        name="pack",
    )(
        block_slots.reshape(-1), destinations.reshape(-1), requests[0].T,
        positions, mass, cell_keys,
    )
    spots = exchange(spot_msg, spot_head + 1, 0)
    shares = swap(mass_msg, n)
    spot_list = spots.reshape(n, spot_rows, BLK)[:, spot_head, :]
    back = pl.pallas_call(
        functools.partial(wind_kernel, (n, room, spot_rows, back_rows)),
        out_shape=jax.ShapeDtypeStruct((n * back_rows, BLK), i32),
        in_specs=[SMEM, VMEM, VMEM],
        out_specs=VMEM,
        scratch_shapes=[pltpu.SMEM((n * (entries // 2) + GROUP,), i32)],
        cost_estimate=pl.CostEstimate(
            flops=blocks * 120 * BLK * MBC * 4, bytes_accessed=blocks * 120 * MBC * 128, transcendentals=0
        ),
        name="wind",
    )(spot_list, spots, winds.reshape(MB, 3 * LEV, MBC))
    back = exchange(back, spot_head, 1)
    moved, turbulence, z_msg = pl.pallas_call(
        functools.partial(move_kernel, (n, blocks, room, back_rows, z_rows)),
        out_shape=(
            jax.ShapeDtypeStruct(positions.shape, f32),
            jax.ShapeDtypeStruct(positions.shape, f32),
            jax.ShapeDtypeStruct((n * z_rows, BLK), f32),
        ),
        in_specs=[SMEM, SMEM, VMEM, VMEM, VMEM, VMEM],
        out_specs=(VMEM, VMEM, VMEM),
        scratch_shapes=[pltpu.VMEM((blocks, BLK), i32), pltpu.VMEM((blocks, BLK), i32)],
        name="move",
    )(spot_place, mass_place, back, positions, velocity, increments)
    heights = exchange(z_msg, room, 2)
    mass_list = shares.reshape(n, mass_rows, BLK)[:, mass_head, :]
    total = pl.pallas_call(
        functools.partial(deposit_kernel, (n, room, mass_rows, z_rows)),
        out_shape=jax.ShapeDtypeStruct((MB, S * LEV, MBC), f32),
        in_specs=[SMEM, VMEM, VMEM],
        out_specs=VMEM,
        scratch_shapes=[pltpu.SMEM((n * max(1, room // 2),), i32)],
        name="deposit",
    )(mass_list, shares, heights)
    concentration = total.reshape(MBR, MBK, S, LEV, MBC)
    return (moved.transpose(1, 0, 2), turbulence.transpose(1, 0, 2), concentration)


def solution(mesh):
    rows = ("lat", "lon")
    in_specs = (
        P("lat", "lon", None, None, None),
        P(rows, None, None),
        P(rows, None, None),
        P(rows, None, None),
        P(rows, None, None),
        P(rows, None, None),
        P(rows, None),
        P(rows, None),
        P(rows, None),
    )
    out_specs = (
        P(rows, None, None),
        P(rows, None, None),
        P("lat", "lon", None, None, None),
    )
    return jax.shard_map(body, mesh=mesh, in_specs=in_specs, out_specs=out_specs, check_vma=False)
```

```python
import functools

import jax
import jax.numpy as jnp
from jax import lax
from jax.experimental import pallas as pl
from jax.experimental.pallas import tpu as pltpu
from jax.sharding import PartitionSpec as P

BY = 8
BX = 16
MBC = 128
LEV = 40
S = 8
BLK = 128
MBR = 4
MBK = 4
Q = 2
MB = MBR * MBK

DECAY = 0.8
KICK = 0.6
STEP = 0.5

FULL = 65535.0
GUST = 6.1
GROUP = 4
BUNCH = 4
VMEM = pl.BlockSpec(memory_space=pltpu.VMEM)
SMEM = pl.BlockSpec(memory_space=pltpu.SMEM)


def up8(rows):
    return -(-rows // 8) * 8


def hat(offset):
    return jnp.maximum(0.0, 1.0 - jnp.abs(offset))


def low(word):
    return (word & 0xFFFF).astype(jnp.float32)


def high(word):
    return lax.shift_right_logical(word, 16).astype(jnp.float32)


def code(value, scale):
    return (value * scale + 0.5).astype(jnp.int32)


def span(count, unroll, step):
    def group(i, carry):
        for j in range(unroll):
            step(i * unroll + j)
        return carry

    lax.fori_loop(0, count // unroll, group, 0)


def pack_kernel(
    dims, slots, targets, requests, positions, mass, keys,
    spot_msg, mass_msg, spot_place, mass_place, spot_count, mass_count, yx, zs,
):
    n, blocks, room, spot_rows, mass_rows = dims
    entries = Q * room
    spot_head = entries + entries // 2
    mass_head = 4 * room + room // 2
    lanes = lax.broadcasted_iota(jnp.int32, (1, BLK), 1)
    spot_msg[...] = jnp.zeros_like(spot_msg)
    mass_msg[...] = jnp.zeros_like(mass_msg)
    yx[...] = code(positions[0], FULL / (BY - 1)) | (code(positions[1], FULL / (BX - 1)) << 16)
    zs[...] = code(positions[2], FULL / (LEV - 1))

    def clear(t, carry):
        spot_count[t] = 0
        mass_count[t] = 0
        return carry

    lax.fori_loop(0, n, clear, 0)

    def one(b):
        slot = slots[b]
        t = slot // Q
        met = requests[slot % Q, t]
        r = spot_count[t]
        spot_count[t] = r + 1
        spot_place[b] = t * entries + r
        base = t * spot_rows
        spot_msg[pl.ds(base + r, 1), :] = yx[pl.ds(b, 1), :]
        z_row = pl.ds(base + entries + r // 2, 1)
        spot_msg[z_row, :] = spot_msg[z_row, :] | (zs[pl.ds(b, 1), :] << (16 * (r & 1)))
        h_row = pl.ds(base + spot_head, 1)
        spot_msg[h_row, :] = jnp.where(
            lanes == r, met, jnp.where(lanes == entries, r + 1, spot_msg[h_row, :])
        )
        d = targets[b]
        q = mass_count[d]
        mass_count[d] = q + 1
        mass_place[b] = d * room + q
        shares = code(mass[b], FULL)
        words = shares[0:4] | (shares[4:8] << 16)
        base = d * mass_rows
        for j in range(4):
            mass_msg[pl.ds(base + 4 * q + j, 1), :] = words[j : j + 1]
        key = keys[pl.ds(b, 1), :]
        k_row = pl.ds(base + 4 * room + q // 2, 1)
        mass_msg[k_row, :] = mass_msg[k_row, :] | (key << (16 * (q & 1)))
        h_row = pl.ds(base + mass_head, 1)
        home = jnp.broadcast_to(key[:, 0:1], (1, BLK)) // MBC
        mass_msg[h_row, :] = jnp.where(
            lanes == q, home, jnp.where(lanes == room, q + 1, mass_msg[h_row, :])
        )

    span(blocks, 4, one)


def list_pairs(n, lane, head, todo, group):
    def source(o, at):
        pairs = (head[o, lane] + 1) // 2

        def put(k, at):
            todo[at] = o * 256 + k
            return at + 1

        return lax.fori_loop(0, pairs, put, at)

    total = lax.fori_loop(0, n, source, 0)
    for j in range(group - 1):
        todo[total + j] = 0
    return total


def wind_kernel(dims, head, spots, tiles, back, todo):
    n, room, spot_rows, back_rows = dims
    entries = Q * room
    total = list_pairs(n, entries, head, todo, GROUP)
    levels = lax.broadcasted_iota(jnp.int32, (LEV, BLK), 0).astype(jnp.float32)
    cols = lax.broadcasted_iota(jnp.int32, (BX, BLK), 0).astype(jnp.float32)

    def sample(o, r, z):
        word = spots[pl.ds(o * spot_rows + r, 1), :]
        y = low(word) * ((BY - 1) / FULL)
        x = high(word) * ((BX - 1) / FULL)
        hx = hat(x - cols)
        flat = jnp.concatenate([hat(y - float(i)) * hx for i in range(BY)], axis=0)
        flat_hi = flat.astype(jnp.bfloat16)
        flat_lo = (flat - flat_hi.astype(jnp.float32)).astype(jnp.bfloat16)
        block = tiles[head[o, r]]
        seen = jnp.dot(
            jnp.concatenate([block, block], axis=1),
            jnp.concatenate([flat_hi, flat_lo], axis=0),
            preferred_element_type=jnp.float32,
        )
        wz = hat(z - levels).astype(jnp.bfloat16).astype(jnp.float32)
        codes = []
        for c in range(3):
            wind = jnp.sum(seen[c * LEV : (c + 1) * LEV] * wz, axis=0, keepdims=True)
            codes.append(code(wind + GUST, FULL / (2 * GUST)))
        return codes[0] | (codes[1] << 16), codes[2]

    def several(i, carry):
        results = []
        for j in range(GROUP):
            item = todo[i * GROUP + j]
            o = item // 256
            k = item % 256
            word = spots[pl.ds(o * spot_rows + entries + k, 1), :]
            first, first_up = sample(o, 2 * k, low(word) * ((LEV - 1) / FULL))
            second, second_up = sample(o, 2 * k + 1, high(word) * ((LEV - 1) / FULL))
            results.append((o * back_rows, k, first, second, first_up | (second_up << 16)))
        for base, k, first, second, up in results:
            back[pl.ds(base + 2 * k, 1), :] = first
            back[pl.ds(base + 2 * k + 1, 1), :] = second
            back[pl.ds(base + entries + k, 1), :] = up
        return carry

    lax.fori_loop(0, (total + GROUP - 1) // GROUP, several, 0)


def move_kernel(
    dims, spot_place, mass_place, back, positions, velocity, increments,
    moved, turbulence, z_msg, yx, zs,
):
    n, blocks, room, back_rows, z_rows = dims
    entries = Q * room
    z_msg[...] = jnp.zeros_like(z_msg)

    def fetch(b):
        place = spot_place[b]
        t = place // entries
        r = place % entries
        yx[pl.ds(b, 1), :] = back[pl.ds(t * back_rows + r, 1), :]
        word = back[pl.ds(t * back_rows + entries + r // 2, 1), :]
        zs[pl.ds(b, 1), :] = lax.shift_right_logical(word, jnp.full_like(word, 16 * (r & 1)))

    span(blocks, 8, fetch)
    winds = (low(yx[...]), high(yx[...]), low(zs[...]))
    for c, top in enumerate((BY - 1.0, BX - 1.0, LEV - 1.0)):
        wind = winds[c] * (2 * GUST / FULL) - GUST
        drift = DECAY * velocity[c] + KICK * increments[c]
        turbulence[c] = drift
        moved[c] = jnp.clip(positions[c] + STEP * (wind + drift), 0.0, top)

    def post(b):
        spot = mass_place[b]
        z_msg[pl.ds((spot // room) * z_rows + spot % room, 1), :] = moved[2, pl.ds(b, 1), :]

    span(blocks, 8, post)


def exchange_kernel(n, n_lon, rows, src, dst, send, recv, local):
    me = lax.axis_index("lat") * n_lon + lax.axis_index("lon")
    barrier = pltpu.get_barrier_semaphore()

    def place(k):
        peer = lax.rem(me + k, n)
        return peer, (peer // n_lon, lax.rem(peer, n_lon))

    def greet(k, carry):
        pl.semaphore_signal(
            barrier, inc=1, device_id=place(k)[1], device_id_type=pl.DeviceIdType.MESH
        )
        return carry

    def copy(k):
        peer, where = place(k)
        return pltpu.make_async_remote_copy(
            src_ref=src.at[peer, pl.ds(0, rows)],
            dst_ref=dst.at[me, pl.ds(0, rows)],
            send_sem=send.at[k],
            recv_sem=recv.at[k],
            device_id=where,
            device_id_type=pl.DeviceIdType.MESH,
        )

    def begin(k, carry):
        copy(k).start()
        return carry

    def finish(k, carry):
        source = lax.rem(me - k + n, n)
        peer, where = place(k)
        copy(k).wait_send()
        pltpu.make_async_remote_copy(
            src_ref=src.at[peer, pl.ds(0, rows)],
            dst_ref=dst.at[source, pl.ds(0, rows)],
            send_sem=send.at[k],
            recv_sem=recv.at[k],
            device_id=where,
            device_id_type=pl.DeviceIdType.MESH,
        ).wait_recv()
        return carry

    own = pltpu.make_async_copy(src.at[me], dst.at[me], local)
    own.start()
    lax.fori_loop(1, n, greet, 0)
    pl.semaphore_wait(barrier, n - 1)
    lax.fori_loop(1, n, begin, 0)
    lax.fori_loop(1, n, finish, 0)
    own.wait()


def exchange(msg, rows, number):
    n_lon = lax.axis_size("lon")
    n = lax.axis_size("lat") * n_lon
    shape = msg.shape
    msg = msg.reshape(n, -1, BLK)
    return pl.pallas_call(
        functools.partial(exchange_kernel, n, n_lon, rows),
        out_shape=jax.ShapeDtypeStruct(msg.shape, msg.dtype),
        in_specs=[VMEM],
        out_specs=VMEM,
        scratch_shapes=[
            pltpu.SemaphoreType.DMA((n,)),
            pltpu.SemaphoreType.DMA((n,)),
            pltpu.SemaphoreType.DMA,
        ],
        compiler_params=pltpu.CompilerParams(collective_id=number, has_side_effects=True),
        name="exchange" + str(number),
    )(msg).reshape(shape)


def deposit_kernel(dims, head, shares, heights, out, todo, filled):
    n, room, mass_rows, z_rows = dims
    most = n * room

    def clear(h, carry):
        filled[h] = 0
        return carry

    lax.fori_loop(0, MB, clear, 0)

    def source(o, carry):
        def put(q, carry):
            h = head[o, q]
            at = filled[h]
            todo[h * most + at] = o * 256 + q
            filled[h] = at + 1
            return carry

        return lax.fori_loop(0, head[o, room], put, carry)

    lax.fori_loop(0, n, source, 0)
    levels = lax.broadcasted_iota(jnp.int32, (LEV, BLK), 0).astype(jnp.float32)
    cells = lax.broadcasted_iota(jnp.int32, (MBC, BLK), 0)

    def spread(h, at):
        valid = at < filled[h]
        item = jnp.where(valid, todo[h * most + at], 0)
        o = item // 256
        q = item % 256
        key = shares[pl.ds(o * mass_rows + 4 * room + q // 2, 1), :]
        key = lax.shift_right_logical(key, jnp.full_like(key, 16 * (q & 1)))
        inside = (key & (MBC - 1)) + jnp.where(valid, 0, MBC)
        vert = hat(heights[pl.ds(o * z_rows + q, 1), :] - levels)
        lows, highs = [], []
        for j in range(4):
            word = shares[pl.ds(o * mass_rows + 4 * q + j, 1), :]
            lows.append((low(word) * (1 / FULL)) * vert)
            highs.append((high(word) * (1 / FULL)) * vert)
        weights = jnp.concatenate(lows + highs, axis=0).astype(jnp.bfloat16)
        picks = jnp.where(inside == cells, 1.0, 0.0).astype(jnp.bfloat16)
        return weights, picks

    def home(h, carry):
        out[h] = jnp.zeros((S * LEV, MBC), jnp.float32)

        def several(i, carry):
            parts = [spread(h, i * BUNCH + j) for j in range(BUNCH)]
            out[h] += lax.dot_general(
                jnp.concatenate([w for w, _ in parts], axis=1),
                jnp.concatenate([p for _, p in parts], axis=1),
                (((1,), (1,)), ((), ())),
                preferred_element_type=jnp.float32,
            )
            return carry

        return lax.fori_loop(0, (filled[h] + BUNCH - 1) // BUNCH, several, carry)

    lax.fori_loop(0, MB, home, 0)


def exchange_kernel(n_lat, n_lon, rows, side_axis, head_row, *refs):
    if side_axis:
        src, side_src, dst, side_dst, head, half = refs[:6]
    else:
        src, dst, half = refs[:3]
    send, recv, local = refs[-3:]
    lat = lax.axis_index("lat")
    lon = lax.axis_index("lon")
    sizes = {"lat": n_lat, "lon": n_lon}
    places = {"lat": lat, "lon": lon}
    firsts = {"main lat": 0, "main lon": n_lat, "side": n_lat + n_lon}
    barrier = pltpu.get_barrier_semaphore()

    def where(axis, k):
        peer = lax.rem(places[axis] + k, sizes[axis])
        return peer, ((peer, lon) if axis == "lat" else (lat, peer))

    def part(ref, axis, index, count):
        if axis == "lat":
            return ref.at[index, :, pl.ds(0, count)]
        return ref.at[:, index, pl.ds(0, count)]

    def copy(name, axis, source, target, count, k, landed):
        peer, device = where(axis, k)
        slot = firsts[name] + k
        return pltpu.make_async_remote_copy(
            src_ref=part(source, axis, peer, count),
            dst_ref=part(target, axis, landed, count),
            send_sem=send.at[slot],
            recv_sem=recv.at[slot],
            device_id=device,
            device_id_type=pl.DeviceIdType.MESH,
        )

    def begin(name, axis, source, target, count):
        own = places[axis]
        pltpu.make_async_copy(
            part(source, axis, own, count),
            part(target, axis, own, count),
            local.at[firsts[name]],
        ).start()
        for k in range(1, sizes[axis]):
            copy(name, axis, source, target, count, k, own).start()

    def finish(name, axis, source, target, count):
        own = places[axis]
        for k in range(1, sizes[axis]):
            landed = lax.rem(own - k + sizes[axis], sizes[axis])
            step = copy(name, axis, source, target, count, k, landed)
            step.wait_send()
            step.wait_recv()
        pltpu.make_async_copy(
            part(source, axis, own, count),
            part(target, axis, own, count),
            local.at[firsts[name]],
        ).wait()

    for axis in ("lat", "lon"):
        for k in range(1, sizes[axis]):
            pl.semaphore_signal(
                barrier, inc=1, device_id=where(axis, k)[1], device_id_type=pl.DeviceIdType.MESH
            )
    pl.semaphore_wait(barrier, n_lat + n_lon - 2)
    main_lat = ("main lat", "lat", src, half, rows)
    main_lon = ("main lon", "lon", half, dst, rows)
    side = ("side", side_axis, side_src, side_dst, side_src.shape[2]) if side_axis else None
    begin(*main_lat)
    if side_axis == "lon":
        begin(*side)
    finish(*main_lat)
    begin(*main_lon)
    if side_axis == "lat":
        begin(*side)
    finish(*main_lon)
    if side_axis == "lon":
        head[...] = dst[:, :, head_row, :]
    if side_axis:
        finish(*side)
    if side_axis == "lat":
        head[...] = side_dst[:, :, head_row, :]


def exchange(msg, rows, number, side=None, side_axis=None, head_row=None):
    n_lat = lax.axis_size("lat")
    n_lon = lax.axis_size("lon")
    shape = msg.shape
    args = [msg.reshape(n_lat, n_lon, -1, BLK)]
    if side_axis:
        args.append(side.reshape(n_lat, n_lon, -1, BLK))
    count = 2 * (n_lat + n_lon)
    made = [jax.ShapeDtypeStruct(each.shape, each.dtype) for each in args]
    if side_axis:
        made.append(jax.ShapeDtypeStruct((n_lat, n_lon, BLK), msg.dtype))
    outs = pl.pallas_call(
        functools.partial(exchange_kernel, n_lat, n_lon, rows, side_axis, head_row),
        out_shape=made,
        in_specs=[VMEM] * len(args),
        out_specs=[VMEM] * len(made),
        scratch_shapes=[
            pltpu.VMEM(args[0].shape, msg.dtype),
            pltpu.SemaphoreType.DMA((count,)),
            pltpu.SemaphoreType.DMA((count,)),
            pltpu.SemaphoreType.DMA((count,)),
        ],
        compiler_params=pltpu.CompilerParams(collective_id=number, has_side_effects=True),
        name="exchange" + str(number),
    )(*args)
    if side_axis:
        return outs[0].reshape(shape), outs[1].reshape(side.shape), outs[2].reshape(-1, BLK)
    return outs[0].reshape(shape)


def body(
    winds, positions, velocity, increments, mass, requests, block_slots, destinations, cell_keys
):
    n = lax.axis_size("lat") * lax.axis_size("lon")
    blocks = positions.shape[0]
    room = 2 * blocks // n
    entries = Q * room
    spot_head = entries + entries // 2
    mass_head = 4 * room + room // 2
    spot_rows = up8(spot_head + 1)
    back_rows = up8(spot_head)
    mass_rows = up8(mass_head + 1)
    z_rows = up8(room)
    i32 = jnp.int32
    f32 = jnp.float32

    positions, velocity, increments = (
        each.transpose(1, 0, 2) for each in (positions, velocity, increments)
    )
    spot_msg, mass_msg, spot_place, mass_place = pl.pallas_call(
        functools.partial(pack_kernel, (n, blocks, room, spot_rows, mass_rows)),
        out_shape=(
            jax.ShapeDtypeStruct((n * spot_rows, BLK), i32),
            jax.ShapeDtypeStruct((n * mass_rows, BLK), i32),
            jax.ShapeDtypeStruct((blocks,), i32),
            jax.ShapeDtypeStruct((blocks,), i32),
        ),
        in_specs=[SMEM, SMEM, SMEM, VMEM, VMEM, VMEM],
        out_specs=(VMEM, VMEM, SMEM, SMEM),
        scratch_shapes=[
            pltpu.SMEM((n,), i32),
            pltpu.SMEM((n,), i32),
            pltpu.VMEM((blocks, BLK), i32),
            pltpu.VMEM((blocks, BLK), i32),
        ],
        name="pack",
    )(
        block_slots.reshape(-1), destinations.reshape(-1), requests[0].T,
        positions, mass, cell_keys,
    )
    spots, shares, spot_list = exchange(spot_msg, spot_head + 1, 0, mass_msg, "lon", spot_head)
    back = pl.pallas_call(
        functools.partial(wind_kernel, (n, room, spot_rows, back_rows)),
        out_shape=jax.ShapeDtypeStruct((n * back_rows, BLK), i32),
        in_specs=[SMEM, VMEM, VMEM],
        out_specs=VMEM,
        scratch_shapes=[pltpu.SMEM((n * (entries // 2) + GROUP,), i32)],
        cost_estimate=pl.CostEstimate(
            flops=blocks * 120 * BLK * MBC * 4, bytes_accessed=blocks * 120 * MBC * 128, transcendentals=0
        ),
        name="wind",
    )(spot_list, spots, winds.reshape(MB, 3 * LEV, MBC))
    back, shares, mass_list = exchange(back, spot_head, 1, shares, "lat", mass_head)
    moved, turbulence, z_msg = pl.pallas_call(
        functools.partial(move_kernel, (n, blocks, room, back_rows, z_rows)),
        out_shape=(
            jax.ShapeDtypeStruct(positions.shape, f32),
            jax.ShapeDtypeStruct(positions.shape, f32),
            jax.ShapeDtypeStruct((n * z_rows, BLK), f32),
        ),
        in_specs=[SMEM, SMEM, VMEM, VMEM, VMEM, VMEM],
        out_specs=(VMEM, VMEM, VMEM),
        scratch_shapes=[pltpu.VMEM((blocks, BLK), i32), pltpu.VMEM((blocks, BLK), i32)],
        name="move",
    )(spot_place, mass_place, back, positions, velocity, increments)
    heights = exchange(z_msg, room, 2)
    total = pl.pallas_call(
        functools.partial(deposit_kernel, (n, room, mass_rows, z_rows)),
        out_shape=jax.ShapeDtypeStruct((MB, S * LEV, MBC), f32),
        in_specs=[SMEM, VMEM, VMEM],
        out_specs=VMEM,
        scratch_shapes=[pltpu.SMEM((MB * n * room + BUNCH,), i32), pltpu.SMEM((MB,), i32)],
        name="deposit",
    )(mass_list, shares, heights)
    concentration = total.reshape(MBR, MBK, S, LEV, MBC)
    return (moved.transpose(1, 0, 2), turbulence.transpose(1, 0, 2), concentration)


def solution(mesh):
    rows = ("lat", "lon")
    in_specs = (
        P("lat", "lon", None, None, None),
        P(rows, None, None),
        P(rows, None, None),
        P(rows, None, None),
        P(rows, None, None),
        P(rows, None, None),
        P(rows, None),
        P(rows, None),
        P(rows, None),
    )
    out_specs = (
        P(rows, None, None),
        P(rows, None, None),
        P("lat", "lon", None, None, None),
    )
    return jax.shard_map(body, mesh=mesh, in_specs=in_specs, out_specs=out_specs, check_vma=False)
```

```python
import functools

import jax
import jax.numpy as jnp
from jax import lax
from jax.experimental import pallas as pl
from jax.experimental.pallas import tpu as pltpu
from jax.sharding import PartitionSpec as P

BY = 8
BX = 16
MBC = 128
LEV = 40
S = 8
BLK = 128
MBR = 4
MBK = 4
Q = 2
MB = MBR * MBK

DECAY = 0.8
KICK = 0.6
STEP = 0.5

FULL = 65535.0
GUST = 6.1
GROUP = 4
BUNCH = 4
SHIFT = 64
VMEM = pl.BlockSpec(memory_space=pltpu.VMEM)
SMEM = pl.BlockSpec(memory_space=pltpu.SMEM)


def up8(rows):
    return -(-rows // 8) * 8


def hat(offset):
    return jnp.maximum(0.0, 1.0 - jnp.abs(offset))


def low(word):
    return (word & 0xFFFF).astype(jnp.float32)


def high(word):
    return lax.shift_right_logical(word, 16).astype(jnp.float32)


def code(value, scale):
    return (value * scale + 0.5).astype(jnp.int32)


def span(count, unroll, step):
    def group(i, carry):
        for j in range(unroll):
            step(i * unroll + j)
        return carry

    lax.fori_loop(0, count // unroll, group, 0)


def pack_kernel(
    dims, slots, targets, requests, positions, mass, keys,
    spot_msg, mass_msg, spot_place, mass_place, spot_count, mass_count, yx, zs,
):
    n, n_lon, blocks, room, spot_rows, mass_rows = dims
    entries = Q * room
    spot_head = entries + entries // 2
    own_row = lax.axis_index("lat") * n_lon
    lanes = lax.broadcasted_iota(jnp.int32, (1, BLK), 1)
    spot_msg[...] = jnp.zeros_like(spot_msg)
    mass_msg[...] = jnp.zeros_like(mass_msg)
    yx[...] = code(positions[0], FULL / (BY - 1)) | (code(positions[1], FULL / (BX - 1)) << 16)
    zs[...] = code(positions[2], FULL / (LEV - 1))

    def clear(t, carry):
        spot_count[t] = 0
        mass_count[t] = 0
        return carry

    lax.fori_loop(0, n, clear, 0)

    def one(b):
        slot = slots[b]
        t = slot // Q
        met = requests[slot % Q, t]
        r = spot_count[t]
        spot_count[t] = r + 1
        spot_place[b] = t * entries + r
        base = t * spot_rows
        spot_msg[pl.ds(base + r, 1), :] = yx[pl.ds(b, 1), :]
        z_row = pl.ds(base + entries + r // 2, 1)
        spot_msg[z_row, :] = spot_msg[z_row, :] | (zs[pl.ds(b, 1), :] << (16 * (r & 1)))
        h_row = pl.ds(base + spot_head, 1)
        spot_msg[h_row, :] = jnp.where(
            lanes == r, met, jnp.where(lanes == entries, r + 1, spot_msg[h_row, :])
        )
        d = targets[b]
        q = mass_count[d]
        mass_count[d] = q + 1
        mass_place[b] = d * room + q
        shares = code(mass[b], FULL)
        words = shares[0:4] | (shares[4:8] << 16)
        base = lax.rem(d - own_row + n, n) * mass_rows
        for j in range(4):
            mass_msg[pl.ds(base + 4 * q + j, 1), :] = words[j : j + 1]
        key = keys[pl.ds(b, 1), :]
        k_row = pl.ds(base + 4 * room + q // 2, 1)
        mass_msg[k_row, :] = mass_msg[k_row, :] | (key << (16 * (q & 1)))
        h_row = pl.ds(d * spot_rows + spot_head, 1)
        home = jnp.broadcast_to(key[:, 0:1], (1, BLK)) // MBC
        spot_msg[h_row, :] = jnp.where(
            lanes == SHIFT + q, home, jnp.where(lanes == SHIFT + room, q + 1, spot_msg[h_row, :])
        )

    span(blocks, 4, one)


def list_pairs(n, lane, head, todo, group):
    def source(o, at):
        pairs = (head[o, lane] + 1) // 2

        def put(k, at):
            todo[at] = o * 256 + k
            return at + 1

        return lax.fori_loop(0, pairs, put, at)

    total = lax.fori_loop(0, n, source, 0)
    for j in range(group - 1):
        todo[total + j] = 0
    return total


def wind_kernel(dims, head, spots, tiles, back, todo):
    n, room, spot_rows, back_rows = dims
    entries = Q * room
    total = list_pairs(n, entries, head, todo, GROUP)
    levels = lax.broadcasted_iota(jnp.int32, (LEV, BLK), 0).astype(jnp.float32)
    cols = lax.broadcasted_iota(jnp.int32, (BX, BLK), 0).astype(jnp.float32)

    def sample(o, r, z):
        word = spots[pl.ds(o * spot_rows + r, 1), :]
        y = low(word) * ((BY - 1) / FULL)
        x = high(word) * ((BX - 1) / FULL)
        hx = hat(x - cols)
        flat = jnp.concatenate([hat(y - float(i)) * hx for i in range(BY)], axis=0)
        flat_hi = flat.astype(jnp.bfloat16)
        flat_lo = (flat - flat_hi.astype(jnp.float32)).astype(jnp.bfloat16)
        block = tiles[head[o, r]]
        seen = jnp.dot(
            jnp.concatenate([block, block], axis=1),
            jnp.concatenate([flat_hi, flat_lo], axis=0),
            preferred_element_type=jnp.float32,
        )
        wz = hat(z - levels).astype(jnp.bfloat16).astype(jnp.float32)
        codes = []
        for c in range(3):
            wind = jnp.sum(seen[c * LEV : (c + 1) * LEV] * wz, axis=0, keepdims=True)
            codes.append(code(wind + GUST, FULL / (2 * GUST)))
        return codes[0] | (codes[1] << 16), codes[2]

    def several(i, carry):
        results = []
        for j in range(GROUP):
            item = todo[i * GROUP + j]
            o = item // 256
            k = item % 256
            word = spots[pl.ds(o * spot_rows + entries + k, 1), :]
            first, first_up = sample(o, 2 * k, low(word) * ((LEV - 1) / FULL))
            second, second_up = sample(o, 2 * k + 1, high(word) * ((LEV - 1) / FULL))
            results.append((o * back_rows, k, first, second, first_up | (second_up << 16)))
        for base, k, first, second, up in results:
            back[pl.ds(base + 2 * k, 1), :] = first
            back[pl.ds(base + 2 * k + 1, 1), :] = second
            back[pl.ds(base + entries + k, 1), :] = up
        return carry

    lax.fori_loop(0, (total + GROUP - 1) // GROUP, several, 0)


def move_kernel(
    dims, spot_place, mass_place, back, positions, velocity, increments,
    moved, turbulence, z_msg, yx, zs,
):
    n, blocks, room, back_rows, z_rows = dims
    entries = Q * room
    z_msg[...] = jnp.zeros_like(z_msg)

    def fetch(b):
        place = spot_place[b]
        t = place // entries
        r = place % entries
        yx[pl.ds(b, 1), :] = back[pl.ds(t * back_rows + r, 1), :]
        word = back[pl.ds(t * back_rows + entries + r // 2, 1), :]
        zs[pl.ds(b, 1), :] = lax.shift_right_logical(word, jnp.full_like(word, 16 * (r & 1)))

    span(blocks, 8, fetch)
    winds = (low(yx[...]), high(yx[...]), low(zs[...]))
    for c, top in enumerate((BY - 1.0, BX - 1.0, LEV - 1.0)):
        wind = winds[c] * (2 * GUST / FULL) - GUST
        drift = DECAY * velocity[c] + KICK * increments[c]
        turbulence[c] = drift
        moved[c] = jnp.clip(positions[c] + STEP * (wind + drift), 0.0, top)

    def post(b):
        spot = mass_place[b]
        z_msg[pl.ds((spot // room) * z_rows + spot % room, 1), :] = moved[2, pl.ds(b, 1), :]

    span(blocks, 8, post)


def deposit_kernel(dims, head, heights, *refs):
    n, n_lat, room, mass_rows, z_rows = dims
    pieces = refs[:n_lat]
    out, shares, todo, filled, landed = refs[n_lat:]
    most = n * room
    n_lon = n // n_lat
    own_row = lax.axis_index("lat") * n_lon
    loads = [
        pltpu.make_async_copy(
            pieces[k], shares.at[pl.ds(k * n_lon * mass_rows, n_lon * mass_rows)], landed.at[k]
        )
        for k in range(n_lat)
    ]
    for load in loads:
        load.start()

    def clear(h, carry):
        filled[h] = 0
        return carry

    lax.fori_loop(0, MB, clear, 0)

    def source(o, carry):
        def put(q, carry):
            h = head[o, SHIFT + q]
            at = filled[h]
            todo[h * most + at] = o * 256 + q
            filled[h] = at + 1
            return carry

        return lax.fori_loop(0, head[o, SHIFT + room], put, carry)

    lax.fori_loop(0, n, source, 0)
    for load in loads:
        load.wait()
    levels = lax.broadcasted_iota(jnp.int32, (LEV, BLK), 0).astype(jnp.float32)
    cells = lax.broadcasted_iota(jnp.int32, (MBC, BLK), 0)

    def spread(h, at):
        valid = at < filled[h]
        item = jnp.where(valid, todo[h * most + at], 0)
        o = item // 256
        q = item % 256
        lag = own_row - (o // n_lon) * n_lon
        base = (lax.rem(lag + n, n) + lax.rem(o, n_lon)) * mass_rows
        key = shares[pl.ds(base + 4 * room + q // 2, 1), :]
        key = lax.shift_right_logical(key, jnp.full_like(key, 16 * (q & 1)))
        inside = (key & (MBC - 1)) + jnp.where(valid, 0, MBC)
        vert = hat(heights[pl.ds(o * z_rows + q, 1), :] - levels)
        lows, highs = [], []
        for j in range(4):
            word = shares[pl.ds(base + 4 * q + j, 1), :]
            lows.append((low(word) * (1 / FULL)) * vert)
            highs.append((high(word) * (1 / FULL)) * vert)
        weights = jnp.concatenate(lows + highs, axis=0).astype(jnp.bfloat16)
        picks = jnp.where(inside == cells, 1.0, 0.0).astype(jnp.bfloat16)
        return weights, picks

    def home(h, carry):
        out[h] = jnp.zeros((S * LEV, MBC), jnp.float32)

        def several(i, carry):
            parts = [spread(h, i * BUNCH + j) for j in range(BUNCH)]
            out[h] += lax.dot_general(
                jnp.concatenate([w for w, _ in parts], axis=1),
                jnp.concatenate([p for _, p in parts], axis=1),
                (((1,), (1,)), ((), ())),
                preferred_element_type=jnp.float32,
            )
            return carry

        return lax.fori_loop(0, (filled[h] + BUNCH - 1) // BUNCH, several, carry)

    lax.fori_loop(0, MB, home, 0)


def exchange_kernel(n_lat, n_lon, rows, head_row, *refs):
    side = head_row is not None
    if side:
        src, side_src, dst, head = refs[:4]
        side_dst = refs[4 : 4 + n_lat]
    else:
        src, dst = refs[:2]
    half, send, recv, side_send, side_recv, local = refs[-6:]
    lat = lax.axis_index("lat")
    lon = lax.axis_index("lon")
    barrier = pltpu.get_barrier_semaphore()
    lat_to = [lax.rem(lat + k, n_lat) for k in range(n_lat)]
    lon_to = [lax.rem(lon + j, n_lon) for j in range(n_lon)]
    lat_from = [lax.rem(lat - k + n_lat, n_lat) for k in range(n_lat)]
    lon_from = [lax.rem(lon - j + n_lon, n_lon) for j in range(n_lon)]
    used = pl.ds(0, rows)

    def remote(source, target, sent, landed, device):
        return pltpu.make_async_remote_copy(
            src_ref=source, dst_ref=target, send_sem=sent, recv_sem=landed,
            device_id=device, device_id_type=pl.DeviceIdType.MESH,
        )

    def lat_copy(k, landed):
        return remote(
            src.at[lat_to[k], :, used], half.at[landed, :, used],
            send.at[k, 0], recv.at[k, 0], (lat_to[k], lon),
        )

    def lon_copy(k, j, landed):
        source = src.at[lat] if k == 0 else half.at[lat_from[k]]
        return remote(
            source.at[lon_to[j], used], dst.at[lat_from[k], landed, used],
            send.at[k, j], recv.at[k, j], (lat, lon_to[j]),
        )

    def own_copy(k):
        source = src.at[lat] if k == 0 else half.at[lat_from[k]]
        return pltpu.make_async_copy(
            source.at[lon, used], dst.at[lat_from[k], lon, used], local.at[k]
        )

    def side_copy(k, j, landed):
        return remote(
            side_src.at[k, lon_to[j]], side_dst[k].at[landed],
            side_send.at[k, j], side_recv.at[k, j], (lat, lon_to[j]),
        )

    def side_own(k):
        return pltpu.make_async_copy(
            side_src.at[k, lon], side_dst[k].at[lon], local.at[n_lat + k]
        )

    for k in range(1, n_lat):
        pl.semaphore_signal(
            barrier, inc=1, device_id=(lat_to[k], lon), device_id_type=pl.DeviceIdType.MESH
        )
    for j in range(1, n_lon):
        pl.semaphore_signal(
            barrier, inc=1, device_id=(lat, lon_to[j]), device_id_type=pl.DeviceIdType.MESH
        )
    pl.semaphore_wait(barrier, n_lat + n_lon - 2)
    for k in range(1, n_lat):
        lat_copy(k, lat).start()
    for k in range(n_lat):
        if k:
            lat_copy(k, lat_from[k]).wait_recv()
        for j in range(1, n_lon):
            lon_copy(k, j, lon).start()
        own_copy(k).start()
        if side:
            for j in range(1, n_lon):
                side_copy(k, j, lon).start()
            side_own(k).start()
    for k in range(n_lat):
        if k:
            lat_copy(k, lat_from[k]).wait_send()
        for j in range(1, n_lon):
            lon_copy(k, j, lon_from[j]).wait_send()
            lon_copy(k, j, lon_from[j]).wait_recv()
        own_copy(k).wait()
    if side:
        head[...] = dst[:, :, head_row, :]
        for k in range(n_lat):
            for j in range(1, n_lon):
                side_copy(k, j, lon_from[j]).wait_send()
                side_copy(k, j, lon_from[j]).wait_recv()
            side_own(k).wait()


def exchange(msg, rows, number, side=None, head_row=None):
    n_lat = lax.axis_size("lat")
    n_lon = lax.axis_size("lon")
    shape = msg.shape
    args = [msg.reshape(n_lat, n_lon, -1, BLK)]
    made = [jax.ShapeDtypeStruct(args[0].shape, msg.dtype)]
    if side is not None:
        args.append(side.reshape(n_lat, n_lon, -1, BLK))
        made.append(jax.ShapeDtypeStruct((n_lat, n_lon, BLK), msg.dtype))
        made += [jax.ShapeDtypeStruct(args[1].shape[1:], msg.dtype)] * n_lat
    outs = pl.pallas_call(
        functools.partial(exchange_kernel, n_lat, n_lon, rows, head_row),
        out_shape=made,
        in_specs=[VMEM] * len(args),
        out_specs=[VMEM] * len(made),
        scratch_shapes=[pltpu.VMEM(args[0].shape, msg.dtype)]
        + [pltpu.SemaphoreType.DMA((n_lat, n_lon))] * 4
        + [pltpu.SemaphoreType.DMA((2 * n_lat,))],
        compiler_params=pltpu.CompilerParams(collective_id=number, has_side_effects=True),
        name="exchange" + str(number),
    )(*args)
    if side is not None:
        return outs[0].reshape(shape), outs[1].reshape(-1, BLK), outs[2:]
    return outs[0].reshape(shape)


def body(
    winds, positions, velocity, increments, mass, requests, block_slots, destinations, cell_keys
):
    n_lat = lax.axis_size("lat")
    n_lon = lax.axis_size("lon")
    n = n_lat * n_lon
    blocks = positions.shape[0]
    room = 2 * blocks // n
    entries = Q * room
    spot_head = entries + entries // 2
    spot_rows = up8(spot_head + 1)
    back_rows = up8(spot_head)
    mass_rows = up8(4 * room + room // 2)
    z_rows = up8(room)
    i32 = jnp.int32
    f32 = jnp.float32

    positions, velocity, increments = (
        each.transpose(1, 0, 2) for each in (positions, velocity, increments)
    )
    spot_msg, mass_msg, spot_place, mass_place = pl.pallas_call(
        functools.partial(pack_kernel, (n, n_lon, blocks, room, spot_rows, mass_rows)),
        out_shape=(
            jax.ShapeDtypeStruct((n * spot_rows, BLK), i32),
            jax.ShapeDtypeStruct((n * mass_rows, BLK), i32),
            jax.ShapeDtypeStruct((blocks,), i32),
            jax.ShapeDtypeStruct((blocks,), i32),
        ),
        in_specs=[SMEM, SMEM, SMEM, VMEM, VMEM, VMEM],
        out_specs=(VMEM, VMEM, SMEM, SMEM),
        scratch_shapes=[
            pltpu.SMEM((n,), i32),
            pltpu.SMEM((n,), i32),
            pltpu.VMEM((blocks, BLK), i32),
            pltpu.VMEM((blocks, BLK), i32),
        ],
        name="pack",
    )(
        block_slots.reshape(-1), destinations.reshape(-1), requests[0].T,
        positions, mass, cell_keys,
    )
    spots, heads, pieces = exchange(spot_msg, spot_head + 1, 0, mass_msg, spot_head)
    pieces = [
        lax.ppermute(piece, "lat", [(i, (i + k) % n_lat) for i in range(n_lat)]) if k else piece
        for k, piece in enumerate(pieces)
    ]
    back = pl.pallas_call(
        functools.partial(wind_kernel, (n, room, spot_rows, back_rows)),
        out_shape=jax.ShapeDtypeStruct((n * back_rows, BLK), i32),
        in_specs=[SMEM, VMEM, VMEM],
        out_specs=VMEM,
        scratch_shapes=[pltpu.SMEM((n * (entries // 2) + GROUP,), i32)],
        cost_estimate=pl.CostEstimate(
            flops=blocks * 120 * BLK * MBC * 4, bytes_accessed=blocks * 120 * MBC * 128, transcendentals=0
        ),
        name="wind",
    )(heads, spots, winds.reshape(MB, 3 * LEV, MBC))
    back = exchange(back, spot_head, 1)
    moved, turbulence, z_msg = pl.pallas_call(
        functools.partial(move_kernel, (n, blocks, room, back_rows, z_rows)),
        out_shape=(
            jax.ShapeDtypeStruct(positions.shape, f32),
            jax.ShapeDtypeStruct(positions.shape, f32),
            jax.ShapeDtypeStruct((n * z_rows, BLK), f32),
        ),
        in_specs=[SMEM, SMEM, VMEM, VMEM, VMEM, VMEM],
        out_specs=(VMEM, VMEM, VMEM),
        scratch_shapes=[pltpu.VMEM((blocks, BLK), i32), pltpu.VMEM((blocks, BLK), i32)],
        name="move",
    )(spot_place, mass_place, back, positions, velocity, increments)
    heights = exchange(z_msg, room, 2)
    total = pl.pallas_call(
        functools.partial(deposit_kernel, (n, n_lat, room, mass_rows, z_rows)),
        out_shape=jax.ShapeDtypeStruct((MB, S * LEV, MBC), f32),
        in_specs=[SMEM, VMEM] + [pl.BlockSpec(memory_space=pl.ANY)] * n_lat,
        out_specs=VMEM,
        scratch_shapes=[
            pltpu.VMEM((n * mass_rows, BLK), i32),
            pltpu.SMEM((MB * n * room + BUNCH,), i32),
            pltpu.SMEM((MB,), i32),
            pltpu.SemaphoreType.DMA((n_lat,)),
        ],
        name="deposit",
    )(heads, heights, *[piece.reshape(-1, BLK) for piece in pieces])
    concentration = total.reshape(MBR, MBK, S, LEV, MBC)
    return (moved.transpose(1, 0, 2), turbulence.transpose(1, 0, 2), concentration)


def solution(mesh):
    rows = ("lat", "lon")
    in_specs = (
        P("lat", "lon", None, None, None),
        P(rows, None, None),
        P(rows, None, None),
        P(rows, None, None),
        P(rows, None, None),
        P(rows, None, None),
        P(rows, None),
        P(rows, None),
        P(rows, None),
    )
    out_specs = (
        P(rows, None, None),
        P(rows, None, None),
        P("lat", "lon", None, None, None),
    )
    return jax.shard_map(body, mesh=mesh, in_specs=in_specs, out_specs=out_specs, check_vma=False)
```

```python
import functools

import jax
import jax.numpy as jnp
from jax import lax
from jax.experimental import pallas as pl
from jax.experimental.pallas import tpu as pltpu
from jax.sharding import PartitionSpec as P

BY = 8
BX = 16
MBC = 128
LEV = 40
S = 8
BLK = 128
MBR = 4
MBK = 4
Q = 2
MB = MBR * MBK

DECAY = 0.8
KICK = 0.6
STEP = 0.5

FULL = 65535.0
GUST = 6.1
GROUP = 4
BUNCH = 4
SHIFT = 64
VMEM = pl.BlockSpec(memory_space=pltpu.VMEM)
SMEM = pl.BlockSpec(memory_space=pltpu.SMEM)


def up8(rows):
    return -(-rows // 8) * 8


def hat(offset):
    return jnp.maximum(0.0, 1.0 - jnp.abs(offset))


def low(word):
    return (word & 0xFFFF).astype(jnp.float32)


def high(word):
    return lax.shift_right_logical(word, 16).astype(jnp.float32)


def code(value, scale):
    return (value * scale + 0.5).astype(jnp.int32)


def span(count, unroll, step):
    def group(i, carry):
        for j in range(unroll):
            step(i * unroll + j)
        return carry

    lax.fori_loop(0, count // unroll, group, 0)


def pack_kernel(
    dims, slots, targets, requests, positions, mass, keys,
    spot_msg, mass_msg, spot_place, mass_place, spot_count, mass_count, yx, zs,
):
    n, n_lon, blocks, room, spot_rows, mass_rows = dims
    entries = Q * room
    spot_head = entries + entries // 2
    own_row = lax.axis_index("lat") * n_lon
    lanes = lax.broadcasted_iota(jnp.int32, (1, BLK), 1)
    spot_msg[...] = jnp.zeros_like(spot_msg)
    mass_msg[...] = jnp.zeros_like(mass_msg)
    yx[...] = code(positions[0], FULL / (BY - 1)) | (code(positions[1], FULL / (BX - 1)) << 16)
    zs[...] = code(positions[2], FULL / (LEV - 1))

    def clear(t, carry):
        spot_count[t] = 0
        mass_count[t] = 0
        return carry

    lax.fori_loop(0, n, clear, 0)

    def one(b):
        slot = slots[b]
        t = slot >> 1
        met = requests[slot & 1, t]
        r = spot_count[t]
        spot_count[t] = r + 1
        spot_place[b] = (t << 8) | r
        base = t * spot_rows
        spot_msg[pl.ds(base + r, 1), :] = yx[pl.ds(b, 1), :]
        z_row = pl.ds(base + entries + (r >> 1), 1)
        spot_msg[z_row, :] = spot_msg[z_row, :] | (zs[pl.ds(b, 1), :] << (16 * (r & 1)))
        h_row = pl.ds(base + spot_head, 1)
        spot_msg[h_row, :] = jnp.where(
            lanes == r, met, jnp.where(lanes == entries, r + 1, spot_msg[h_row, :])
        )
        d = targets[b]
        q = mass_count[d]
        mass_count[d] = q + 1
        mass_place[b] = (d << 8) | q
        shares = code(mass[b], FULL)
        words = shares[0:4] | (shares[4:8] << 16)
        base = lax.rem(d - own_row + n, n) * mass_rows
        for j in range(4):
            mass_msg[pl.ds(base + 4 * q + j, 1), :] = words[j : j + 1]
        key = keys[pl.ds(b, 1), :]
        k_row = pl.ds(base + 4 * room + (q >> 1), 1)
        mass_msg[k_row, :] = mass_msg[k_row, :] | (key << (16 * (q & 1)))
        h_row = pl.ds(d * spot_rows + spot_head, 1)
        home = jnp.broadcast_to(key[:, 0:1], (1, BLK)) >> 7
        spot_msg[h_row, :] = jnp.where(
            lanes == SHIFT + q, home, jnp.where(lanes == SHIFT + room, q + 1, spot_msg[h_row, :])
        )

    span(blocks, 4, one)


def list_pairs(n, lane, head, todo, group):
    def source(o, at):
        pairs = (head[o, lane] + 1) >> 1

        def put(k, at):
            todo[at] = o * 256 + k
            return at + 1

        return lax.fori_loop(0, pairs, put, at)

    total = lax.fori_loop(0, n, source, 0)
    for j in range(group - 1):
        todo[total + j] = 0
    return total


def wind_kernel(dims, head, spots, tiles, back, todo):
    n, room, spot_rows, back_rows = dims
    entries = Q * room
    total = list_pairs(n, entries, head, todo, GROUP)
    levels = lax.broadcasted_iota(jnp.int32, (LEV, BLK), 0).astype(jnp.float32)
    cols = lax.broadcasted_iota(jnp.int32, (BX, BLK), 0).astype(jnp.float32)

    def sample(o, r, z):
        word = spots[pl.ds(o * spot_rows + r, 1), :]
        y = low(word) * ((BY - 1) / FULL)
        x = high(word) * ((BX - 1) / FULL)
        hx = hat(x - cols)
        flat = jnp.concatenate([hat(y - float(i)) * hx for i in range(BY)], axis=0)
        flat_hi = flat.astype(jnp.bfloat16)
        flat_lo = (flat - flat_hi.astype(jnp.float32)).astype(jnp.bfloat16)
        block = tiles[head[o, r]]
        seen = jnp.dot(
            jnp.concatenate([block, block], axis=1),
            jnp.concatenate([flat_hi, flat_lo], axis=0),
            preferred_element_type=jnp.float32,
        )
        wz = hat(z - levels).astype(jnp.bfloat16).astype(jnp.float32)
        codes = []
        for c in range(3):
            wind = jnp.sum(seen[c * LEV : (c + 1) * LEV] * wz, axis=0, keepdims=True)
            codes.append(code(wind + GUST, FULL / (2 * GUST)))
        return codes[0] | (codes[1] << 16), codes[2]

    def several(i, carry):
        results = []
        for j in range(GROUP):
            item = todo[i * GROUP + j]
            o = item >> 8
            k = item & 255
            word = spots[pl.ds(o * spot_rows + entries + k, 1), :]
            first, first_up = sample(o, 2 * k, low(word) * ((LEV - 1) / FULL))
            second, second_up = sample(o, 2 * k + 1, high(word) * ((LEV - 1) / FULL))
            results.append((o * back_rows, k, first, second, first_up | (second_up << 16)))
        for base, k, first, second, up in results:
            back[pl.ds(base + 2 * k, 1), :] = first
            back[pl.ds(base + 2 * k + 1, 1), :] = second
            back[pl.ds(base + entries + k, 1), :] = up
        return carry

    lax.fori_loop(0, (total + GROUP - 1) // GROUP, several, 0)


def move_kernel(
    dims, spot_place, mass_place, back, positions, velocity, increments,
    moved, turbulence, z_msg, yx, zs,
):
    n, blocks, room, back_rows, z_rows = dims
    entries = Q * room
    z_msg[...] = jnp.zeros_like(z_msg)

    def fetch(b):
        place = spot_place[b]
        t = place >> 8
        r = place & 255
        yx[pl.ds(b, 1), :] = back[pl.ds(t * back_rows + r, 1), :]
        word = back[pl.ds(t * back_rows + entries + (r >> 1), 1), :]
        zs[pl.ds(b, 1), :] = lax.shift_right_logical(word, jnp.full_like(word, 16 * (r & 1)))

    span(blocks, 8, fetch)
    winds = (low(yx[...]), high(yx[...]), low(zs[...]))
    for c, top in enumerate((BY - 1.0, BX - 1.0, LEV - 1.0)):
        wind = winds[c] * (2 * GUST / FULL) - GUST
        drift = DECAY * velocity[c] + KICK * increments[c]
        turbulence[c] = drift
        moved[c] = jnp.clip(positions[c] + STEP * (wind + drift), 0.0, top)

    def post(b):
        spot = mass_place[b]
        z_msg[pl.ds((spot >> 8) * z_rows + (spot & 255), 1), :] = moved[2, pl.ds(b, 1), :]

    span(blocks, 8, post)


def deposit_kernel(dims, head, heights, *refs):
    n, n_lat, room, mass_rows, z_rows = dims
    pieces = refs[:n_lat]
    out, shares, todo, filled, landed = refs[n_lat:]
    most = n * room
    n_lon = n // n_lat
    own_row = lax.axis_index("lat") * n_lon
    loads = [
        pltpu.make_async_copy(
            pieces[k], shares.at[pl.ds(k * n_lon * mass_rows, n_lon * mass_rows)], landed.at[k]
        )
        for k in range(n_lat)
    ]
    for load in loads:
        load.start()

    def clear(h, carry):
        filled[h] = 0
        return carry

    lax.fori_loop(0, MB, clear, 0)

    def source(o, carry):
        lag = own_row - (o // n_lon) * n_lon
        label = (((lax.rem(lag + n, n) + lax.rem(o, n_lon)) << 12) | o) << 8

        def put(q, carry):
            h = head[o, SHIFT + q]
            at = filled[h]
            todo[h * most + at] = label | q
            filled[h] = at + 1
            return carry

        return lax.fori_loop(0, head[o, SHIFT + room], put, carry)

    lax.fori_loop(0, n, source, 0)
    for load in loads:
        load.wait()
    levels = lax.broadcasted_iota(jnp.int32, (LEV, BLK), 0).astype(jnp.float32)
    cells = lax.broadcasted_iota(jnp.int32, (MBC, BLK), 0)

    def spread(h, at):
        valid = at < filled[h]
        item = jnp.where(valid, todo[h * most + at], 0)
        o = (item >> 8) & 0xFFF
        q = item & 255
        base = (item >> 20) * mass_rows
        key = shares[pl.ds(base + 4 * room + (q >> 1), 1), :]
        key = lax.shift_right_logical(key, jnp.full_like(key, 16 * (q & 1)))
        inside = (key & (MBC - 1)) + jnp.where(valid, 0, MBC)
        vert = hat(heights[pl.ds(o * z_rows + q, 1), :] - levels)
        lows, highs = [], []
        for j in range(4):
            word = shares[pl.ds(base + 4 * q + j, 1), :]
            lows.append((low(word) * (1 / FULL)) * vert)
            highs.append((high(word) * (1 / FULL)) * vert)
        weights = jnp.concatenate(lows + highs, axis=0).astype(jnp.bfloat16)
        picks = jnp.where(inside == cells, 1.0, 0.0).astype(jnp.bfloat16)
        return weights, picks

    def home(h, carry):
        out[h] = jnp.zeros((S * LEV, MBC), jnp.float32)

        def several(i, carry):
            parts = [spread(h, i * BUNCH + j) for j in range(BUNCH)]
            out[h] += lax.dot_general(
                jnp.concatenate([w for w, _ in parts], axis=1),
                jnp.concatenate([p for _, p in parts], axis=1),
                (((1,), (1,)), ((), ())),
                preferred_element_type=jnp.float32,
            )
            return carry

        return lax.fori_loop(0, (filled[h] + BUNCH - 1) // BUNCH, several, carry)

    lax.fori_loop(0, MB, home, 0)


def exchange_kernel(n_lat, n_lon, rows, head_row, *refs):
    split = head_row is not None
    side = not split and len(refs) > 8
    if split:
        src, side_src, dst, head = refs[:4]
        side_dst = refs[4 : 4 + n_lat]
    elif side:
        src, side_src = refs[0], refs[1 : 1 + n_lat]
        dst, side_dst = refs[1 + n_lat], refs[2 + n_lat : 2 + 2 * n_lat]
    else:
        src, dst = refs[:2]
    half, send, recv, side_send, side_recv, local = refs[-6:]
    lat = lax.axis_index("lat")
    lon = lax.axis_index("lon")
    barrier = pltpu.get_barrier_semaphore()
    lat_to = [lax.rem(lat + k, n_lat) for k in range(n_lat)]
    lon_to = [lax.rem(lon + j, n_lon) for j in range(n_lon)]
    lat_from = [lax.rem(lat - k + n_lat, n_lat) for k in range(n_lat)]
    lon_from = [lax.rem(lon - j + n_lon, n_lon) for j in range(n_lon)]
    used = pl.ds(0, rows)

    def remote(source, target, sent, landed, device):
        return pltpu.make_async_remote_copy(
            src_ref=source, dst_ref=target, send_sem=sent, recv_sem=landed,
            device_id=device, device_id_type=pl.DeviceIdType.MESH,
        )

    def lat_copy(k, landed):
        return remote(
            src.at[lat_to[k], :, used], half.at[landed, :, used],
            send.at[k, 0], recv.at[k, 0], (lat_to[k], lon),
        )

    def lon_copy(k, j, landed):
        source = src.at[lat] if k == 0 else half.at[lat_from[k]]
        return remote(
            source.at[lon_to[j], used], dst.at[lat_from[k], landed, used],
            send.at[k, j], recv.at[k, j], (lat, lon_to[j]),
        )

    def own_copy(k):
        source = src.at[lat] if k == 0 else half.at[lat_from[k]]
        return pltpu.make_async_copy(
            source.at[lon, used], dst.at[lat_from[k], lon, used], local.at[k]
        )

    def side_copy(k, j, landed):
        return remote(
            side_src[k].at[lon_to[j]], side_dst[k].at[landed],
            side_send.at[k, j], side_recv.at[k, j], (lat, lon_to[j]),
        )

    def side_own(k):
        if split:
            return pltpu.make_async_copy(side_src.at[k], side_dst[k], local.at[n_lat + k])
        return pltpu.make_async_copy(
            side_src[k].at[lon], side_dst[k].at[lon], local.at[n_lat + k]
        )

    for k in range(1, n_lat):
        pl.semaphore_signal(
            barrier, inc=1, device_id=(lat_to[k], lon), device_id_type=pl.DeviceIdType.MESH
        )
    for j in range(1, n_lon):
        pl.semaphore_signal(
            barrier, inc=1, device_id=(lat, lon_to[j]), device_id_type=pl.DeviceIdType.MESH
        )
    pl.semaphore_wait(barrier, n_lat + n_lon - 2)
    for k in range(1, n_lat):
        lat_copy(k, lat).start()
    if side:
        for k in range(n_lat):
            for j in range(1, n_lon):
                side_copy(k, j, lon).start()
    if side or split:
        for k in range(n_lat):
            side_own(k).start()
    for k in range(n_lat):
        if k:
            lat_copy(k, lat_from[k]).wait_recv()
        for j in range(1, n_lon):
            lon_copy(k, j, lon).start()
        own_copy(k).start()
    for k in range(n_lat):
        if k:
            lat_copy(k, lat_from[k]).wait_send()
        for j in range(1, n_lon):
            lon_copy(k, j, lon_from[j]).wait_send()
            lon_copy(k, j, lon_from[j]).wait_recv()
        own_copy(k).wait()
    if split:
        head[...] = dst[:, :, head_row, :]
    for k in range(n_lat if side or split else 0):
        if side:
            for j in range(1, n_lon):
                side_copy(k, j, lon_from[j]).wait_send()
                side_copy(k, j, lon_from[j]).wait_recv()
        side_own(k).wait()


def exchange(msg, rows, number, side=None, head_row=None):
    n_lat = lax.axis_size("lat")
    n_lon = lax.axis_size("lon")
    shape = msg.shape
    args = [msg.reshape(n_lat, n_lon, -1, BLK)]
    made = [jax.ShapeDtypeStruct(args[0].shape, msg.dtype)]
    if head_row is not None:
        args.append(side.reshape(n_lat, n_lon, -1, BLK))
        made.append(jax.ShapeDtypeStruct((n_lat, n_lon, BLK), msg.dtype))
        made += [jax.ShapeDtypeStruct(args[1].shape[1:], msg.dtype)] * n_lat
    elif side is not None:
        args += side
        made += [jax.ShapeDtypeStruct(each.shape, each.dtype) for each in side]
    outs = pl.pallas_call(
        functools.partial(exchange_kernel, n_lat, n_lon, rows, head_row),
        out_shape=made,
        in_specs=[VMEM] * len(args),
        out_specs=[VMEM] * len(made),
        scratch_shapes=[pltpu.VMEM(args[0].shape, msg.dtype)]
        + [pltpu.SemaphoreType.DMA((n_lat, n_lon))] * 4
        + [pltpu.SemaphoreType.DMA((2 * n_lat,))],
        compiler_params=pltpu.CompilerParams(collective_id=number, has_side_effects=True),
        name="exchange" + str(number),
    )(*args)
    if head_row is not None:
        return outs[0].reshape(shape), outs[1].reshape(-1, BLK), outs[2:]
    if side is not None:
        return outs[0].reshape(shape), outs[1:]
    return outs[0].reshape(shape)


def body(
    winds, positions, velocity, increments, mass, requests, block_slots, destinations, cell_keys
):
    n_lat = lax.axis_size("lat")
    n_lon = lax.axis_size("lon")
    n = n_lat * n_lon
    blocks = positions.shape[0]
    room = 2 * blocks // n
    entries = Q * room
    spot_head = entries + entries // 2
    spot_rows = up8(spot_head + 1)
    back_rows = up8(spot_head)
    mass_rows = up8(4 * room + room // 2)
    z_rows = up8(room)
    i32 = jnp.int32
    f32 = jnp.float32

    positions, velocity, increments = (
        each.transpose(1, 0, 2) for each in (positions, velocity, increments)
    )
    spot_msg, mass_msg, spot_place, mass_place = pl.pallas_call(
        functools.partial(pack_kernel, (n, n_lon, blocks, room, spot_rows, mass_rows)),
        out_shape=(
            jax.ShapeDtypeStruct((n * spot_rows, BLK), i32),
            jax.ShapeDtypeStruct((n * mass_rows, BLK), i32),
            jax.ShapeDtypeStruct((blocks,), i32),
            jax.ShapeDtypeStruct((blocks,), i32),
        ),
        in_specs=[SMEM, SMEM, SMEM, VMEM, VMEM, VMEM],
        out_specs=(VMEM, VMEM, SMEM, SMEM),
        scratch_shapes=[
            pltpu.SMEM((n,), i32),
            pltpu.SMEM((n,), i32),
            pltpu.VMEM((blocks, BLK), i32),
            pltpu.VMEM((blocks, BLK), i32),
        ],
        name="pack",
    )(
        block_slots.reshape(-1), destinations.reshape(-1), requests[0].T,
        positions, mass, cell_keys,
    )
    spots, heads, pieces = exchange(spot_msg, spot_head + 1, 0, mass_msg, spot_head)
    pieces = [
        lax.ppermute(piece, "lat", [(i, (i + k) % n_lat) for i in range(n_lat)]) if k else piece
        for k, piece in enumerate(pieces)
    ]
    back = pl.pallas_call(
        functools.partial(wind_kernel, (n, room, spot_rows, back_rows)),
        out_shape=jax.ShapeDtypeStruct((n * back_rows, BLK), i32),
        in_specs=[SMEM, VMEM, VMEM],
        out_specs=VMEM,
        scratch_shapes=[pltpu.SMEM((n * (entries // 2) + GROUP,), i32)],
        cost_estimate=pl.CostEstimate(
            flops=blocks * 120 * BLK * MBC * 4, bytes_accessed=blocks * 120 * MBC * 128, transcendentals=0
        ),
        name="wind",
    )(heads, spots, winds.reshape(MB, 3 * LEV, MBC))
    back, pieces = exchange(back, spot_head, 1, pieces)
    moved, turbulence, z_msg = pl.pallas_call(
        functools.partial(move_kernel, (n, blocks, room, back_rows, z_rows)),
        out_shape=(
            jax.ShapeDtypeStruct(positions.shape, f32),
            jax.ShapeDtypeStruct(positions.shape, f32),
            jax.ShapeDtypeStruct((n * z_rows, BLK), f32),
        ),
        in_specs=[SMEM, SMEM, VMEM, VMEM, VMEM, VMEM],
        out_specs=(VMEM, VMEM, VMEM),
        scratch_shapes=[pltpu.VMEM((blocks, BLK), i32), pltpu.VMEM((blocks, BLK), i32)],
        name="move",
    )(spot_place, mass_place, back, positions, velocity, increments)
    heights = exchange(z_msg, room, 2)
    total = pl.pallas_call(
        functools.partial(deposit_kernel, (n, n_lat, room, mass_rows, z_rows)),
        out_shape=jax.ShapeDtypeStruct((MB, S * LEV, MBC), f32),
        in_specs=[SMEM, VMEM] + [pl.BlockSpec(memory_space=pl.ANY)] * n_lat,
        out_specs=VMEM,
        scratch_shapes=[
            pltpu.VMEM((n * mass_rows, BLK), i32),
            pltpu.SMEM((MB * n * room + BUNCH,), i32),
            pltpu.SMEM((MB,), i32),
            pltpu.SemaphoreType.DMA((n_lat,)),
        ],
        name="deposit",
    )(heads, heights, *[piece.reshape(-1, BLK) for piece in pieces])
    concentration = total.reshape(MBR, MBK, S, LEV, MBC)
    return (moved.transpose(1, 0, 2), turbulence.transpose(1, 0, 2), concentration)


def solution(mesh):
    rows = ("lat", "lon")
    in_specs = (
        P("lat", "lon", None, None, None),
        P(rows, None, None),
        P(rows, None, None),
        P(rows, None, None),
        P(rows, None, None),
        P(rows, None, None),
        P(rows, None),
        P(rows, None),
        P(rows, None),
    )
    out_specs = (
        P(rows, None, None),
        P(rows, None, None),
        P("lat", "lon", None, None, None),
    )
    return jax.shard_map(body, mesh=mesh, in_specs=in_specs, out_specs=out_specs, check_vma=False)
```

```python
import functools

import jax
import jax.numpy as jnp
from jax import lax
from jax.experimental import pallas as pl
from jax.experimental.pallas import tpu as pltpu
from jax.sharding import PartitionSpec as P

BY = 8
BX = 16
MBC = 128
LEV = 40
S = 8
BLK = 128
MBR = 4
MBK = 4
Q = 2
MB = MBR * MBK

DECAY = 0.8
KICK = 0.6
STEP = 0.5

FULL = 65535.0
GUST = 6.1
GROUP = 4
BUNCH = 4
SHIFT = 64
VMEM = pl.BlockSpec(memory_space=pltpu.VMEM)
SMEM = pl.BlockSpec(memory_space=pltpu.SMEM)


def up8(rows):
    return -(-rows // 8) * 8


def hat(offset):
    return jnp.maximum(0.0, 1.0 - jnp.abs(offset))


def low(word):
    return (word & 0xFFFF).astype(jnp.float32)


def high(word):
    return lax.shift_right_logical(word, 16).astype(jnp.float32)


def code(value, scale):
    return (value * scale + 0.5).astype(jnp.int32)


def span(count, unroll, step):
    def group(i, carry):
        for j in range(unroll):
            step(i * unroll + j)
        return carry

    lax.fori_loop(0, count // unroll, group, 0)


def pack_kernel(
    dims, slots, targets, requests, positions, mass, keys,
    spot_msg, mass_msg, spot_place, mass_place, spot_count, mass_count, yx, zs,
):
    n, n_lon, blocks, room, spot_rows, mass_rows = dims
    entries = Q * room
    spot_head = entries + entries // 2
    own_row = lax.axis_index("lat") * n_lon
    lanes = lax.broadcasted_iota(jnp.int32, (1, BLK), 1)
    spot_msg[...] = jnp.zeros_like(spot_msg)
    mass_msg[...] = jnp.zeros_like(mass_msg)
    yx[...] = code(positions[0], FULL / (BY - 1)) | (code(positions[1], FULL / (BX - 1)) << 16)
    zs[...] = code(positions[2], FULL / (LEV - 1))

    def clear(t, carry):
        spot_count[t] = 0
        mass_count[t] = 0
        return carry

    lax.fori_loop(0, n, clear, 0)

    def one(b):
        slot = slots[b]
        t = slot >> 1
        met = requests[slot & 1, t]
        r = spot_count[t]
        spot_count[t] = r + 1
        spot_place[b] = (t << 8) | r
        base = t * spot_rows
        spot_msg[pl.ds(base + r, 1), :] = yx[pl.ds(b, 1), :]
        z_row = pl.ds(base + entries + (r >> 1), 1)
        spot_msg[z_row, :] = spot_msg[z_row, :] | (zs[pl.ds(b, 1), :] << (16 * (r & 1)))
        h_row = pl.ds(base + spot_head, 1)
        spot_msg[h_row, :] = jnp.where(
            lanes == r, met, jnp.where(lanes == entries, r + 1, spot_msg[h_row, :])
        )
        d = targets[b]
        q = mass_count[d]
        mass_count[d] = q + 1
        mass_place[b] = (d << 8) | q
        shares = code(mass[b], FULL)
        words = shares[0:4] | (shares[4:8] << 16)
        base = lax.rem(d - own_row + n, n) * mass_rows
        for j in range(4):
            mass_msg[pl.ds(base + 4 * q + j, 1), :] = words[j : j + 1]
        key = keys[pl.ds(b, 1), :]
        k_row = pl.ds(base + 4 * room + (q >> 1), 1)
        mass_msg[k_row, :] = mass_msg[k_row, :] | (key << (16 * (q & 1)))
        h_row = pl.ds(d * spot_rows + spot_head, 1)
        home = jnp.broadcast_to(key[:, 0:1], (1, BLK)) >> 7
        spot_msg[h_row, :] = jnp.where(
            lanes == SHIFT + q, home, jnp.where(lanes == SHIFT + room, q + 1, spot_msg[h_row, :])
        )

    span(blocks, 4, one)


def list_pairs(n, lane, head, todo, group):
    def source(o, at):
        pairs = (head[o, lane] + 1) >> 1

        def put(k, at):
            todo[at] = o * 256 + k
            return at + 1

        return lax.fori_loop(0, pairs, put, at)

    total = lax.fori_loop(0, n, source, 0)
    for j in range(group - 1):
        todo[total + j] = 0
    return total


def wind_kernel(dims, head, spots, tiles, back, todo):
    n, room, spot_rows, back_rows = dims
    entries = Q * room
    total = list_pairs(n, entries, head, todo, GROUP)
    levels = lax.broadcasted_iota(jnp.int32, (LEV, BLK), 0).astype(jnp.float32)
    cols = lax.broadcasted_iota(jnp.int32, (BX, BLK), 0).astype(jnp.float32)

    def sample(o, r, z):
        word = spots[pl.ds(o * spot_rows + r, 1), :]
        y = low(word) * ((BY - 1) / FULL)
        x = high(word) * ((BX - 1) / FULL)
        hx = hat(x - cols)
        flat = jnp.concatenate([hat(y - float(i)) * hx for i in range(BY)], axis=0)
        flat_hi = flat.astype(jnp.bfloat16)
        flat_lo = (flat - flat_hi.astype(jnp.float32)).astype(jnp.bfloat16)
        block = tiles[head[o, r]]
        seen = jnp.dot(
            jnp.concatenate([block, block], axis=1),
            jnp.concatenate([flat_hi, flat_lo], axis=0),
            preferred_element_type=jnp.float32,
        )
        wz = hat(z - levels).astype(jnp.bfloat16).astype(jnp.float32)
        codes = []
        for c in range(3):
            wind = jnp.sum(seen[c * LEV : (c + 1) * LEV] * wz, axis=0, keepdims=True)
            codes.append(code(wind + GUST, FULL / (2 * GUST)))
        return codes[0] | (codes[1] << 16), codes[2]

    def several(i, carry):
        results = []
        for j in range(GROUP):
            item = todo[i * GROUP + j]
            o = item >> 8
            k = item & 255
            word = spots[pl.ds(o * spot_rows + entries + k, 1), :]
            first, first_up = sample(o, 2 * k, low(word) * ((LEV - 1) / FULL))
            second, second_up = sample(o, 2 * k + 1, high(word) * ((LEV - 1) / FULL))
            results.append((o * back_rows, k, first, second, first_up | (second_up << 16)))
        for base, k, first, second, up in results:
            back[pl.ds(base + 2 * k, 1), :] = first
            back[pl.ds(base + 2 * k + 1, 1), :] = second
            back[pl.ds(base + entries + k, 1), :] = up
        return carry

    lax.fori_loop(0, (total + GROUP - 1) // GROUP, several, 0)


def move_kernel(
    dims, spot_place, mass_place, back, positions, velocity, increments,
    moved, turbulence, z_msg, yx, zs,
):
    n, blocks, room, back_rows, z_rows = dims
    entries = Q * room
    z_msg[...] = jnp.zeros_like(z_msg)

    def fetch(b):
        place = spot_place[b]
        t = place >> 8
        r = place & 255
        yx[pl.ds(b, 1), :] = back[pl.ds(t * back_rows + r, 1), :]
        word = back[pl.ds(t * back_rows + entries + (r >> 1), 1), :]
        zs[pl.ds(b, 1), :] = lax.shift_right_logical(word, jnp.full_like(word, 16 * (r & 1)))

    span(blocks, 8, fetch)
    winds = (low(yx[...]), high(yx[...]), low(zs[...]))
    for c, top in enumerate((BY - 1.0, BX - 1.0, LEV - 1.0)):
        wind = winds[c] * (2 * GUST / FULL) - GUST
        drift = DECAY * velocity[c] + KICK * increments[c]
        turbulence[c] = drift
        moved[c] = jnp.clip(positions[c] + STEP * (wind + drift), 0.0, top)

    def post(b):
        spot = mass_place[b]
        z_msg[pl.ds((spot >> 8) * z_rows + (spot & 255), 1), :] = moved[2, pl.ds(b, 1), :]

    span(blocks, 8, post)


def deposit_kernel(dims, head, heights, *refs):
    n, n_lat, room, mass_rows, z_rows = dims
    pieces = refs[:n_lat]
    out, shares, todo, filled, landed = refs[n_lat:]
    most = n * room
    n_lon = n // n_lat
    own_row = lax.axis_index("lat") * n_lon
    loads = [
        pltpu.make_async_copy(
            pieces[k], shares.at[pl.ds(k * n_lon * mass_rows, n_lon * mass_rows)], landed.at[k]
        )
        for k in range(n_lat)
    ]
    for load in loads:
        load.start()

    def clear(h, carry):
        filled[h] = 0
        return carry

    lax.fori_loop(0, MB, clear, 0)

    def source(o, carry):
        lag = own_row - (o // n_lon) * n_lon
        label = (((lax.rem(lag + n, n) + lax.rem(o, n_lon)) << 12) | o) << 8

        def put(q, carry):
            h = head[o, SHIFT + q]
            at = filled[h]
            todo[h * most + at] = label | q
            filled[h] = at + 1
            return carry

        return lax.fori_loop(0, head[o, SHIFT + room], put, carry)

    lax.fori_loop(0, n, source, 0)
    for load in loads:
        load.wait()
    levels = lax.broadcasted_iota(jnp.int32, (LEV, BLK), 0).astype(jnp.float32)
    cells = lax.broadcasted_iota(jnp.int32, (MBC, BLK), 0)

    def spread(h, at):
        valid = at < filled[h]
        item = jnp.where(valid, todo[h * most + at], 0)
        o = (item >> 8) & 0xFFF
        q = item & 255
        base = (item >> 20) * mass_rows
        key = shares[pl.ds(base + 4 * room + (q >> 1), 1), :]
        key = lax.shift_right_logical(key, jnp.full_like(key, 16 * (q & 1)))
        inside = (key & (MBC - 1)) + jnp.where(valid, 0, MBC)
        vert = hat(heights[pl.ds(o * z_rows + q, 1), :] - levels)
        lows, highs = [], []
        for j in range(4):
            word = shares[pl.ds(base + 4 * q + j, 1), :]
            lows.append((low(word) * (1 / FULL)) * vert)
            highs.append((high(word) * (1 / FULL)) * vert)
        weights = jnp.concatenate(lows + highs, axis=0).astype(jnp.bfloat16)
        picks = jnp.where(inside == cells, 1.0, 0.0).astype(jnp.bfloat16)
        return weights, picks

    def home(h, carry):
        out[h] = jnp.zeros((S * LEV, MBC), jnp.float32)

        def several(i, carry):
            parts = [spread(h, i * BUNCH + j) for j in range(BUNCH)]
            out[h] += lax.dot_general(
                jnp.concatenate([w for w, _ in parts], axis=1),
                jnp.concatenate([p for _, p in parts], axis=1),
                (((1,), (1,)), ((), ())),
                preferred_element_type=jnp.float32,
            )
            return carry

        return lax.fori_loop(0, (filled[h] + BUNCH - 1) // BUNCH, several, carry)

    lax.fori_loop(0, MB, home, 0)


def exchange_kernel(n_lat, n_lon, rows, head_row, *refs):
    split = head_row is not None
    side = not split and len(refs) > 8
    if split:
        src, side_src, dst, head = refs[:4]
        side_dst = refs[4 : 4 + n_lat]
    elif side:
        src, side_src = refs[0], refs[1 : 1 + n_lat]
        dst, side_dst = refs[1 + n_lat], refs[2 + n_lat : 2 + 2 * n_lat]
    else:
        src, dst = refs[:2]
    half, send, recv, side_send, side_recv, local = refs[-6:]
    lat = lax.axis_index("lat")
    lon = lax.axis_index("lon")
    barrier = pltpu.get_barrier_semaphore()
    lat_to = [lax.rem(lat + k, n_lat) for k in range(n_lat)]
    lon_to = [lax.rem(lon + j, n_lon) for j in range(n_lon)]
    lat_from = [lax.rem(lat - k + n_lat, n_lat) for k in range(n_lat)]
    lon_from = [lax.rem(lon - j + n_lon, n_lon) for j in range(n_lon)]
    used = pl.ds(0, rows)

    def remote(source, target, sent, landed, device):
        return pltpu.make_async_remote_copy(
            src_ref=source, dst_ref=target, send_sem=sent, recv_sem=landed,
            device_id=device, device_id_type=pl.DeviceIdType.MESH,
        )

    def lat_copy(k, landed):
        return remote(
            src.at[lat_to[k], :, used], half.at[landed, :, used],
            send.at[k, 0], recv.at[k, 0], (lat_to[k], lon),
        )

    def lon_copy(k, j, landed):
        source = src.at[lat] if k == 0 else half.at[lat_from[k]]
        return remote(
            source.at[lon_to[j], used], dst.at[lat_from[k], landed, used],
            send.at[k, j], recv.at[k, j], (lat, lon_to[j]),
        )

    def own_copy(k):
        source = src.at[lat] if k == 0 else half.at[lat_from[k]]
        return pltpu.make_async_copy(
            source.at[lon, used], dst.at[lat_from[k], lon, used], local.at[k]
        )

    def side_copy(k, j, landed):
        return remote(
            side_src[k].at[lon_to[j]], side_dst[k].at[landed],
            side_send.at[k, j], side_recv.at[k, j], (lat, lon_to[j]),
        )

    def side_own(k):
        if split:
            return pltpu.make_async_copy(side_src.at[k], side_dst[k], local.at[n_lat + k])
        return pltpu.make_async_copy(
            side_src[k].at[lon], side_dst[k].at[lon], local.at[n_lat + k]
        )

    for k in range(1, n_lat):
        pl.semaphore_signal(
            barrier, inc=1, device_id=(lat_to[k], lon), device_id_type=pl.DeviceIdType.MESH
        )
    for j in range(1, n_lon):
        pl.semaphore_signal(
            barrier, inc=1, device_id=(lat, lon_to[j]), device_id_type=pl.DeviceIdType.MESH
        )
    pl.semaphore_wait(barrier, n_lat + n_lon - 2)
    for k in range(1, n_lat):
        lat_copy(k, lat).start()
    if side:
        for k in range(n_lat):
            for j in range(1, n_lon):
                side_copy(k, j, lon).start()
    if side or split:
        for k in range(n_lat):
            side_own(k).start()
    for k in range(n_lat):
        if k:
            lat_copy(k, lat_from[k]).wait_recv()
        for j in range(1, n_lon):
            lon_copy(k, j, lon).start()
        own_copy(k).start()
    for k in range(n_lat):
        if k:
            lat_copy(k, lat_from[k]).wait_send()
        for j in range(1, n_lon):
            lon_copy(k, j, lon_from[j]).wait_send()
            lon_copy(k, j, lon_from[j]).wait_recv()
        own_copy(k).wait()
    if split:
        head[...] = dst[:, :, head_row, :]
    for k in range(n_lat if side or split else 0):
        if side:
            for j in range(1, n_lon):
                side_copy(k, j, lon_from[j]).wait_send()
                side_copy(k, j, lon_from[j]).wait_recv()
        side_own(k).wait()


def exchange(msg, rows, number, side=None, head_row=None):
    n_lat = lax.axis_size("lat")
    n_lon = lax.axis_size("lon")
    shape = msg.shape
    args = [msg.reshape(n_lat, n_lon, -1, BLK)]
    made = [jax.ShapeDtypeStruct(args[0].shape, msg.dtype)]
    if head_row is not None:
        args.append(side.reshape(n_lat, n_lon, -1, BLK))
        made.append(jax.ShapeDtypeStruct((n_lat, n_lon, BLK), msg.dtype))
        made += [jax.ShapeDtypeStruct(args[1].shape[1:], msg.dtype)] * n_lat
    elif side is not None:
        args += side
        made += [jax.ShapeDtypeStruct(each.shape, each.dtype) for each in side]
    outs = pl.pallas_call(
        functools.partial(exchange_kernel, n_lat, n_lon, rows, head_row),
        out_shape=made,
        in_specs=[VMEM] * len(args),
        out_specs=[VMEM] * len(made),
        scratch_shapes=[pltpu.VMEM(args[0].shape, msg.dtype)]
        + [pltpu.SemaphoreType.DMA((n_lat, n_lon))] * 4
        + [pltpu.SemaphoreType.DMA((2 * n_lat,))],
        compiler_params=pltpu.CompilerParams(collective_id=number, has_side_effects=True),
        name="exchange" + str(number),
    )(*args)
    if head_row is not None:
        return outs[0].reshape(shape), outs[1].reshape(-1, BLK), outs[2:]
    if side is not None:
        return outs[0].reshape(shape), outs[1:]
    return outs[0].reshape(shape)


def body(
    winds, positions, velocity, increments, mass, requests, block_slots, destinations, cell_keys
):
    n_lat = lax.axis_size("lat")
    n_lon = lax.axis_size("lon")
    n = n_lat * n_lon
    blocks = positions.shape[0]
    room = 2 * blocks // n
    entries = Q * room
    spot_head = entries + entries // 2
    spot_rows = up8(spot_head + 1)
    back_rows = up8(spot_head)
    mass_rows = up8(4 * room + room // 2)
    z_rows = up8(room)
    i32 = jnp.int32
    f32 = jnp.float32

    positions, velocity, increments = (
        each.transpose(1, 0, 2) for each in (positions, velocity, increments)
    )
    spot_msg, mass_msg, spot_place, mass_place = pl.pallas_call(
        functools.partial(pack_kernel, (n, n_lon, blocks, room, spot_rows, mass_rows)),
        out_shape=(
            jax.ShapeDtypeStruct((n * spot_rows, BLK), i32),
            jax.ShapeDtypeStruct((n * mass_rows, BLK), i32),
            jax.ShapeDtypeStruct((blocks,), i32),
            jax.ShapeDtypeStruct((blocks,), i32),
        ),
        in_specs=[SMEM, SMEM, SMEM, VMEM, VMEM, VMEM],
        out_specs=(VMEM, VMEM, SMEM, SMEM),
        scratch_shapes=[
            pltpu.SMEM((n,), i32),
            pltpu.SMEM((n,), i32),
            pltpu.VMEM((blocks, BLK), i32),
            pltpu.VMEM((blocks, BLK), i32),
        ],
        name="pack",
    )(
        block_slots.reshape(-1), destinations.reshape(-1), requests[0].T,
        positions, mass, cell_keys,
    )
    spots, heads, pieces = exchange(spot_msg, spot_head + 1, 0, mass_msg, spot_head)
    pieces = [
        lax.ppermute(piece, "lat", [(i, (i + k) % n_lat) for i in range(n_lat)]) if k else piece
        for k, piece in enumerate(pieces)
    ]
    back = pl.pallas_call(
        functools.partial(wind_kernel, (n, room, spot_rows, back_rows)),
        out_shape=jax.ShapeDtypeStruct((n * back_rows, BLK), i32),
        in_specs=[SMEM, VMEM, VMEM],
        out_specs=VMEM,
        scratch_shapes=[pltpu.SMEM((n * (entries // 2) + GROUP,), i32)],
        cost_estimate=pl.CostEstimate(
            flops=blocks * 120 * BLK * MBC * 4, bytes_accessed=blocks * 120 * MBC * 128, transcendentals=0
        ),
        name="wind",
    )(heads, spots, winds.reshape(MB, 3 * LEV, MBC))
    back = exchange(back, spot_head, 1)
    moved, turbulence, z_msg = pl.pallas_call(
        functools.partial(move_kernel, (n, blocks, room, back_rows, z_rows)),
        out_shape=(
            jax.ShapeDtypeStruct(positions.shape, f32),
            jax.ShapeDtypeStruct(positions.shape, f32),
            jax.ShapeDtypeStruct((n * z_rows, BLK), f32),
        ),
        in_specs=[SMEM, SMEM, VMEM, VMEM, VMEM, VMEM],
        out_specs=(VMEM, VMEM, VMEM),
        scratch_shapes=[pltpu.VMEM((blocks, BLK), i32), pltpu.VMEM((blocks, BLK), i32)],
        name="move",
    )(spot_place, mass_place, back, positions, velocity, increments)
    heights, pieces = exchange(z_msg, room, 2, pieces)
    total = pl.pallas_call(
        functools.partial(deposit_kernel, (n, n_lat, room, mass_rows, z_rows)),
        out_shape=jax.ShapeDtypeStruct((MB, S * LEV, MBC), f32),
        in_specs=[SMEM, VMEM] + [pl.BlockSpec(memory_space=pl.ANY)] * n_lat,
        out_specs=VMEM,
        scratch_shapes=[
            pltpu.VMEM((n * mass_rows, BLK), i32),
            pltpu.SMEM((MB * n * room + BUNCH,), i32),
            pltpu.SMEM((MB,), i32),
            pltpu.SemaphoreType.DMA((n_lat,)),
        ],
        name="deposit",
    )(heads, heights, *[piece.reshape(-1, BLK) for piece in pieces])
    concentration = total.reshape(MBR, MBK, S, LEV, MBC)
    return (moved.transpose(1, 0, 2), turbulence.transpose(1, 0, 2), concentration)


def solution(mesh):
    rows = ("lat", "lon")
    in_specs = (
        P("lat", "lon", None, None, None),
        P(rows, None, None),
        P(rows, None, None),
        P(rows, None, None),
        P(rows, None, None),
        P(rows, None, None),
        P(rows, None),
        P(rows, None),
        P(rows, None),
    )
    out_specs = (
        P(rows, None, None),
        P(rows, None, None),
        P("lat", "lon", None, None, None),
    )
    return jax.shard_map(body, mesh=mesh, in_specs=in_specs, out_specs=out_specs, check_vma=False)
```
